256 devices in a mesh: ga: 4 (over x), gx: 8 (over y, z_lo), gy: 8 (over z_hi, core).
Axes of the slice: x: 4, y: 4, z: 8 (z_hi: 4, z_lo: 2; z = z_hi * 2 + z_lo), core: 2. Of those that a mesh axis runs over, the one named last changes fastest.
Arguments:
- value: float32 [16, 32, 32, 6400], P('ga', 'gx', 'gy'), may hold values from -4 to 12
- gust: float32 [16, 32], P('ga', 'gx'), may hold values from 0.02 to 2.1, as said below
Outputs:
- value_next: float32 [16, 32, 32, 6400], P('ga', 'gx', 'gy')
- time_step: float32 [1], replicated
The draws below stay inside these ranges and needn't reach their ends.
Inputs may be any that keep to these rules, and one draw needn't show every extreme that they name: gust is positive.
All inputs are finite; a program needn't handle non-finite values.
Results may differ from the reference program's by a relative error of at most 0.00002.
Values sent between devices are 32-bit elements; how exact they have to be, the bound alone decides.
No kernel may reach another device: no remote copies, remote signals or barrier semaphores. Data moves between devices by JAX's collectives and lax.ppermute only.
A program may use at most 128 MiB of HBM per device.

```python
import math
import jax
import jax.numpy as jnp
from jax import lax

N4 = 40
N5 = 40
N6 = 4
N1 = 16
N2 = 32
N3 = 32


def centred_units(count):
    return (jnp.arange(count, dtype=jnp.int32).astype(jnp.float32) + 0.5) / count * 2.0 - 1.0


def draw_value(key, part):
    width = N4 * N5 * N6
    unit_one = centred_units(N1).reshape(N1, 1, 1, 1)
    unit_two = centred_units(N2).reshape(1, N2, 1, 1)
    heading = (-math.pi + jnp.arange(N3, dtype=jnp.int32).astype(jnp.float32) * (2.0 * math.pi / N3)).reshape(1, 1, N3, 1)
    positions = jnp.arange(width, dtype=jnp.int32)
    unit_four = ((positions // (N5 * N6)).astype(jnp.float32) + 0.5) / N4 * 2.0 - 1.0
    unit_five = ((positions // N6 % N5).astype(jnp.float32) + 0.5) / N5 * 2.0 - 1.0
    unit_six = ((positions % N6).astype(jnp.float32) + 0.5) / N6 * 2.0 - 1.0
    params = jax.random.uniform(jax.random.fold_in(key, 11), (12,), jnp.float32, -1.0, 1.0)
    slopes = jax.random.uniform(jax.random.fold_in(key, 12), (3,), jnp.float32, 0.5, 1.0)
    centre_one = 2.0 * params[0]
    centre_two = 2.0 * params[1]
    pos_one = 5.0 * unit_one
    pos_two = 5.0 * unit_two
    distance = jnp.sqrt((pos_one - centre_one) ** 2 + (pos_two - centre_two) ** 2 + 0.25) - 1.5
    turn_amp = 0.4
    rough = 0.08 * jnp.clip(jax.random.normal(jax.random.fold_in(key, 13), (N1, N2, N3, 1), jnp.float32), -1.75, 1.75)
    fine = 0.025 * jnp.clip(jax.random.normal(jax.random.fold_in(key, 14), (N1, N2, N3, width), jnp.float32), -1.75, 1.75)
    turning = turn_amp * jnp.cos(heading - math.pi * params[2])
    speed_part = 0.1 * slopes[0] * unit_four + 0.08 * slopes[1] * unit_five + 0.015 * slopes[2] * unit_six
    modulation = 1.0 + 0.6 * jnp.sin(math.pi * (params[6] * unit_one + params[7] * unit_two) + math.pi * params[8])
    bump_one = 0.8 * params[9]
    bump_two = 0.8 * params[10]
    bump = jnp.exp(-((unit_one - bump_one) ** 2 + (unit_two - bump_two) ** 2) / 0.08)
    bump = bump * (1.0 + 0.15 * unit_four - 0.1 * unit_five + 0.02 * unit_six)
    return distance + turning + speed_part * modulation + bump + rough + fine


def draw_gust(key, part):
    key_tilt, key_rough = jax.random.split(key)
    tilt = jax.random.uniform(key_tilt, (2,), jnp.float32, -0.75, 0.75)
    rows = (jnp.arange(N1).astype(jnp.float32) + 0.5) / N1 * 2.0 - 1.0
    cols = (jnp.arange(N2).astype(jnp.float32) + 0.5) / N2 * 2.0 - 1.0
    ramp = jnp.exp(tilt[0] * rows[:, None] + tilt[1] * cols[None, :])
    rough = jax.random.uniform(key_rough, (N1, N2), jnp.float32, 0.5, 1.5)
    return 0.3 * rough * ramp


def setup_inputs(seed: int = 0) -> dict:
    key_of = jax.random.split(jax.random.key(seed), 3)
    value = draw_value(jax.random.fold_in(key_of[2], 71), 0)
    gust = draw_gust(jax.random.fold_in(key_of[2], 71), 0)
    return {"value": value, "gust": gust}


turn_max = 1.0
accel_max = 0.5
other_accel = 0.4
spin_max = 0.3
smooth_width = 0.25
courant = 0.5
weno_eps = 1e-06
omega_step = 0.05
half_span = 5.0

def extend_linear(field, axis):
    count = field.shape[axis]
    first = lax.slice_in_dim(field, 0, 1, axis=axis)
    second = lax.slice_in_dim(field, 1, 2, axis=axis)
    last = lax.slice_in_dim(field, count - 1, count, axis=axis)
    before = lax.slice_in_dim(field, count - 2, count - 1, axis=axis)
    return jnp.concatenate([3.0 * first - 2.0 * second, 2.0 * first - second, field, 2.0 * last - before, 3.0 * last - 2.0 * before], axis=axis)

def extend_wrap(field, axis):
    count = field.shape[axis]
    return jnp.concatenate([lax.slice_in_dim(field, count - 2, count, axis=axis), field, lax.slice_in_dim(field, 0, 2, axis=axis)], axis=axis)

def weno_core(back_two, back_one, here_diff, ahead_one, curve_back, curve_here, curve_ahead):
    base = 0.5 * (back_one + here_diff)
    ratio_minus = (weno_eps + curve_back * curve_back) / (weno_eps + curve_here * curve_here)
    ratio_plus = (weno_eps + curve_ahead * curve_ahead) / (weno_eps + curve_here * curve_here)
    weight_minus = 1.0 / (1.0 + 2.0 * ratio_minus * ratio_minus)
    weight_plus = 1.0 / (1.0 + 2.0 * ratio_plus * ratio_plus)
    minus = base - 0.5 * weight_minus * (back_two - 2.0 * back_one + here_diff)
    plus = base - 0.5 * weight_plus * (ahead_one - 2.0 * here_diff + back_one)
    return (minus, plus)

def weno_padded(padded, axis, count, spacing):
    diffs = (lax.slice_in_dim(padded, 1, count + 4, axis=axis) - lax.slice_in_dim(padded, 0, count + 3, axis=axis)) / spacing
    curves = (lax.slice_in_dim(diffs, 1, count + 3, axis=axis) - lax.slice_in_dim(diffs, 0, count + 2, axis=axis)) / spacing

    def piece(array, start):
        return lax.slice_in_dim(array, start, start + count, axis=axis)
    return weno_core(piece(diffs, 0), piece(diffs, 1), piece(diffs, 2), piece(diffs, 3), piece(curves, 0), piece(curves, 1), piece(curves, 2))

def weno_block(centre, axis, count, spacing):
    shaped = centre.reshape(centre.shape[0], centre.shape[1], N4, N5, N6)
    minus, plus = weno_padded(extend_linear(shaped, axis), axis, count, spacing)
    return (minus.reshape(centre.shape), plus.reshape(centre.shape))

def rates_and_hamiltonian(mean_grads, pos_one, pos_two, heading, speed_own, speed_other, turn_rate, gust_here):
    grad_one, grad_two, grad_three, grad_four, grad_five, grad_six = mean_grads
    switch = grad_one * pos_two - grad_two * pos_one - grad_three
    switch_root = jnp.sqrt(switch * switch + smooth_width ** 2)
    switch_unit = switch / switch_root
    push_root = jnp.sqrt(grad_one * grad_one + grad_two * grad_two + smooth_width ** 2)
    root_four = jnp.sqrt(grad_four * grad_four + smooth_width ** 2)
    root_five = jnp.sqrt(grad_five * grad_five + smooth_width ** 2)
    root_six = jnp.sqrt(grad_six * grad_six + smooth_width ** 2)
    drift_one = speed_other * jnp.cos(heading) - speed_own
    drift_two = speed_other * jnp.sin(heading)
    rates = (jnp.abs(drift_one) + turn_max * jnp.abs(switch_unit * pos_two) + gust_here * jnp.abs(grad_one) / push_root, jnp.abs(drift_two) + turn_max * jnp.abs(switch_unit * pos_one) + gust_here * jnp.abs(grad_two) / push_root, jnp.abs(turn_rate) + turn_max * jnp.abs(switch_unit), accel_max * jnp.abs(grad_four) / root_four, other_accel * jnp.abs(grad_five) / root_five, spin_max * jnp.abs(grad_six) / root_six)
    hamil = grad_one * drift_one + grad_two * drift_two + grad_three * turn_rate + turn_max * switch_root + accel_max * root_four - other_accel * root_five - spin_max * root_six - gust_here * push_root
    return (rates, hamil)

def reference(value, gust):
    step_a = 2.0 * half_span / N1
    step_b = 2.0 * half_span / N2
    step_c = 2.0 * math.pi / N3
    step_four = 1.0 / N4
    step_five = 1.0 / N5
    extended = extend_linear(value, 0)
    positions = jnp.arange(N4 * N5 * N6, dtype=jnp.int32)
    speed_own = 0.5 + ((positions // (N5 * N6)).astype(jnp.float32) + 0.5) * step_four
    speed_other = 0.5 + ((positions // N6 % N5).astype(jnp.float32) + 0.5) * step_five
    turn_rate = ((positions % N6).astype(jnp.float32) - 0.5 * (N6 - 1)) * omega_step
    pos_two = (-half_span + (jnp.arange(N2, dtype=jnp.int32).astype(jnp.float32) + 0.5) * step_b).reshape(N2, 1, 1)
    heading = (-math.pi + jnp.arange(N3, dtype=jnp.int32).astype(jnp.float32) * step_c).reshape(1, N3, 1)
    indices = jnp.arange(N1, dtype=jnp.int32)

    def plane(index):
        block = lax.dynamic_slice_in_dim(extended, index, 5, 0)
        centre = block[2]
        first_minus, first_plus = weno_padded(block, 0, 1, step_a)
        pairs = [(first_minus[0], first_plus[0]), weno_padded(extend_linear(centre, 0), 0, N2, step_b), weno_padded(extend_wrap(centre, 1), 1, N3, step_c), weno_block(centre, 2, N4, step_four), weno_block(centre, 3, N5, step_five), weno_block(centre, 4, N6, omega_step)]
        pos_one = -half_span + (index.astype(jnp.float32) + 0.5) * step_a
        gust_here = lax.dynamic_slice_in_dim(gust, index, 1, 0).reshape(N2, 1, 1)
        mean_grads = [0.5 * (minus + plus) for minus, plus in pairs]
        rates, hamil = rates_and_hamiltonian(mean_grads, pos_one, pos_two, heading, speed_own, speed_other, turn_rate, gust_here)
        return (pairs, rates, hamil)

    def plane_speeds(index):
        pairs, rates, hamil = plane(index)
        return jnp.stack([jnp.max(rate) for rate in rates])
    speeds = lax.optimization_barrier(jnp.max(lax.map(plane_speeds, indices), axis=0))
    spacing = jnp.array([step_a, step_b, step_c, step_four, step_five, omega_step], jnp.float32)
    time_step = courant / jnp.sum(speeds / spacing)

    def plane_update(index):
        pairs, rates, hamil = plane(index)
        smoothing = speeds[0] * (pairs[0][1] - pairs[0][0])
        for number in range(1, 6):
            smoothing = smoothing + speeds[number] * (pairs[number][1] - pairs[number][0])
        numeric = hamil - 0.5 * smoothing
        current = lax.dynamic_slice_in_dim(value, index, 1, 0)[0]
        return current - time_step * numeric
    value_next = lax.map(plane_update, indices)
    return (value_next, time_step.reshape(1))
```

```python
import math

import jax
import jax.numpy as jnp
import numpy as np
from jax import lax
from jax.experimental import pallas as pl
from jax.experimental.pallas import tpu as pltpu
from jax.sharding import PartitionSpec as P

N4 = 40
N5 = 40
N6 = 4
WIDTH = N4 * N5 * N6
LANES = 128
PAIRS = WIDTH // (2 * LANES)

turn_max = 1.0
accel_max = 0.5
other_accel = 0.4
spin_max = 0.3
smooth_width = 0.25
courant = 0.5
weno_eps = 1e-06
omega_step = 0.05
half_span = 5.0
soft = smooth_width**2


def load(ref, lead, j):
    return jnp.concatenate(
        [
            ref[(*lead, slice(None), pl.ds(256 * j, 128))],
            ref[(*lead, slice(None), pl.ds(256 * j + 128, 128))],
        ],
        axis=0,
    )


def store(ref, lead, j, x):
    ref[(*lead, slice(None), pl.ds(256 * j, 128))] = x[:4]
    ref[(*lead, slice(None), pl.ds(256 * j + 128, 128))] = x[4:]


def squared_curve(curve, eps):
    e = curve * curve + eps
    return e * e


def weno(d_back, d_here, s_back, s_here, s_ahead, q_back, q_here, q_ahead, scale):
    u_minus = (s_here - s_back) * (q_here / (q_here + (q_back + q_back)))
    u_plus = (s_ahead - s_here) * (q_here / (q_here + (q_ahead + q_ahead)))
    mean = scale * ((d_back + d_here) - 0.5 * (u_minus + u_plus))
    return mean, u_minus - u_plus


def column(values, spacing):
    eps = weno_eps * spacing**4
    d = [b - a for a, b in zip(values[:-1], values[1:])]
    s = [b - a for a, b in zip(d[:-1], d[1:])]
    q = [squared_curve(x, eps) for x in s]
    return [
        weno(d[i + 1], d[i + 2], s[i], s[i + 1], s[i + 2], q[i], q[i + 1], q[i + 2], 0.5 / spacing)
        for i in range(len(values) - 4)
    ]


def inner_kernel(v_ref, code_ref, g4_ref, g5_ref, g6_ref, h_ref, most_ref):
    x = [load(v_ref, (0,), j) for j in range(PAIRS)]
    lane = lax.broadcasted_iota(jnp.int32, (8, LANES), 1)
    upper = lax.broadcasted_iota(jnp.int32, (8, LANES), 0) < 4

    def up4(r):
        y = [pltpu.roll(a, 4, 0) for a in r]
        return [jnp.where(upper, y[k], y[(k + 1) % PAIRS]) for k in range(PAIRS)]

    def down4(r):
        y = [pltpu.roll(a, 4, 0) for a in r]
        return [jnp.where(upper, y[k - 1], y[k]) for k in range(PAIRS)]

    def ahead(a, stride):
        n = stride % LANES
        r = [pltpu.roll(y, LANES - n, 1) for y in a]
        if stride == 1:
            return r
        u = up4(r)
        near, far = (r, u) if stride < LANES else (u, r[1:] + r[:1])
        return [jnp.where(lane < LANES - n, near[k], far[k]) for k in range(PAIRS)]

    def back(a, stride):
        n = stride % LANES
        r = [pltpu.roll(y, n, 1) for y in a]
        if stride == 1:
            return r
        u = down4(r)
        near, far = (r, u) if stride < LANES else (u, r[-1:] + r[:-1])
        return [jnp.where(lane >= n, near[k], far[k]) for k in range(PAIRS)]

    total = [None] * PAIRS
    most = []
    for stride, spacing, weight, g_ref, which in (
        (N5 * N6, 1.0 / N4, accel_max, g4_ref, 0),
        (N6, 1.0 / N5, -other_accel, g5_ref, 1),
        (1, omega_step, -spin_max, g6_ref, 2),
    ):
        eps = weno_eps * spacing**4
        if which < 2:
            codes = [code_ref[which, pl.ds(8 * k, 8), :] for k in range(PAIRS)]
        else:
            place = lane % N6
            codes = [jnp.where(place == 0, -1, jnp.where(place == N6 - 1, 1, 0))] * PAIRS
        d = [b - a for a, b in zip(x, ahead(x, stride))]
        before = [a - b for a, b in zip(x, back(x, stride))]
        d_here = [jnp.where(c > 0, b, a) for c, a, b in zip(codes, d, before)]
        d_back = [jnp.where(c < 0, a, b) for c, a, b in zip(codes, d, before)]
        s = [a - b for a, b in zip(d_here, d_back)]
        s_ahead = ahead(s, stride)
        s_back = back(s, stride)
        if which == 2:
            s_ahead = [jnp.where(c > 0, 0.0, a) for c, a in zip(codes, s_ahead)]
            s_back = [jnp.where(c < 0, 0.0, a) for c, a in zip(codes, s_back)]
        peak = None
        for k in range(PAIRS):
            mean, diff = weno(
                d_back[k],
                d_here[k],
                s_back[k],
                s[k],
                s_ahead[k],
                squared_curve(s_back[k], eps),
                squared_curve(s[k], eps),
                squared_curve(s_ahead[k], eps),
                0.5 / spacing,
            )
            store(g_ref, (0,), k, diff)
            square = mean * mean
            peak = square if peak is None else jnp.maximum(peak, square)
            y = square + soft
            root = weight * (y * lax.rsqrt(y))
            total[k] = root if total[k] is None else total[k] + root
        most.append(peak)
    for k in range(PAIRS):
        store(h_ref, (0,), k, total[k])

    @pl.when(pl.program_id(0) == 0)
    def _():
        for i in range(3):
            most_ref[i] = most[i]

    @pl.when(pl.program_id(0) > 0)
    def _():
        for i in range(3):
            most_ref[i] = jnp.maximum(most_ref[i], most[i])


def rows_kernel(
    step_a, step_c, scal_ref, v_ref, low_ref, high_ref, turn_ref, h_ref, drift_ref, rate_ref,
    p1_ref, m_ref, hp_ref, g1_ref, g3_ref,
):
    eps_c = weno_eps * step_c**4
    place = lax.broadcasted_iota(jnp.int32, (8, LANES), 0) % 4
    at_low = scal_ref[24] > 0.0
    at_high = scal_ref[25] > 0.0

    @pl.loop(0, 4)
    def _(b):
        pos_two = scal_ref[4 + b]
        for j in range(v_ref.shape[-1] // 256):
            v = [load(v_ref, (a, b), j) for a in range(4)]
            low = [load(low_ref, (a, b), j) for a in range(2)]
            high = [load(high_ref, (a, b), j) for a in range(2)]
            low = [
                jnp.where(at_low, 3.0 * v[0] - 2.0 * v[1], low[0]),
                jnp.where(at_low, 2.0 * v[0] - v[1], low[1]),
            ]
            high = [
                jnp.where(at_high, 2.0 * v[3] - v[2], high[0]),
                jnp.where(at_high, 3.0 * v[3] - 2.0 * v[2], high[1]),
            ]
            firsts = column(low + v + high, step_a)
            drift = load(drift_ref, (0,), j)
            rate = load(rate_ref, (), j)
            for a in range(4):
                x = v[a]
                ghost = load(turn_ref, (a, b), j)
                x_m2 = jnp.where(place < 2, ghost, pltpu.roll(x, 2, 0))
                x_m1 = jnp.where(place == 0, pltpu.roll(ghost, 7, 0), pltpu.roll(x, 1, 0))
                x_p1 = jnp.where(place == 3, pltpu.roll(ghost, 1, 0), pltpu.roll(x, 7, 0))
                x_p2 = jnp.where(place >= 2, ghost, pltpu.roll(x, 6, 0))
                (p3, g3), = column([x_m2, x_m1, x, x_p1, x_p2], step_c)
                p1, g1 = firsts[a]
                store(g1_ref, (a, b), j, g1)
                store(g3_ref, (a, b), j, g3)
                store(p1_ref, (a, b), j, p1)
                store(m_ref, (a, b), j, p1 * pos_two - p3)
                store(hp_ref, (a, b), j, p1 * drift + p3 * rate + load(h_ref, (a, b), j))


def last_kernel(
    step_b, scal_ref, v_ref, low_ref, high_ref, p1_ref, m_ref, hp_ref, drift_ref,
    h_ref, g2_ref, most_ref,
):
    at_low = scal_ref[26] > 0.0
    at_high = scal_ref[27] > 0.0

    @pl.when(pl.program_id(0) == 0)
    def _():
        most_ref[...] = jnp.zeros_like(most_ref)

    @pl.loop(0, 4)
    def _(a):
        pos_one = scal_ref[a]
        most = [most_ref[i] for i in range(3)]
        for j in range(v_ref.shape[-1] // 256):
            v = [load(v_ref, (a, b), j) for b in range(4)]
            low = [load(low_ref, (a, b), j) for b in range(2)]
            high = [load(high_ref, (a, b), j) for b in range(2)]
            low = [
                jnp.where(at_low, 3.0 * v[0] - 2.0 * v[1], low[0]),
                jnp.where(at_low, 2.0 * v[0] - v[1], low[1]),
            ]
            high = [
                jnp.where(at_high, 2.0 * v[3] - v[2], high[0]),
                jnp.where(at_high, 3.0 * v[3] - 2.0 * v[2], high[1]),
            ]
            drift_one = load(drift_ref, (0,), j)
            drift_two = load(drift_ref, (1,), j)
            for b, (p2, g2) in enumerate(column(low + v + high, step_b)):
                gust = scal_ref[8 + 4 * a + b]
                store(g2_ref, (a, b), j, g2)
                p1 = load(p1_ref, (a, b), j)
                switch = load(m_ref, (a, b), j) - p2 * pos_one
                square = switch * switch
                y = square + soft
                r = lax.rsqrt(y)
                unit = jnp.abs(switch) * r
                push = (p1 * p1 + p2 * p2) + soft
                k = lax.rsqrt(push)
                wind = gust * k
                one = jnp.abs(drift_one) + unit * jnp.abs(scal_ref[4 + b]) + jnp.abs(p1) * wind
                two = jnp.abs(drift_two) + unit * jnp.abs(pos_one) + jnp.abs(p2) * wind
                most = [
                    jnp.maximum(most[0], one),
                    jnp.maximum(most[1], two),
                    jnp.maximum(most[2], square),
                ]
                hamil = load(hp_ref, (a, b), j) + p2 * drift_two + y * r - wind * push
                store(h_ref, (a, b), j, hamil)
        for i in range(3):
            most_ref[i] = most[i]


def edge_codes():
    flat = np.arange(WIDTH).reshape(WIDTH // LANES, 1, LANES)
    flat = np.broadcast_to(flat, (WIDTH // LANES, 4, LANES)).reshape(-1, LANES)
    codes = []
    for stride, count in ((N5 * N6, N4), (N6, N5)):
        place = flat // stride % count
        codes.append(np.where(place == 0, -1, np.where(place == count - 1, 1, 0)))
    return np.stack(codes).astype(np.int32)


def exchange(low, high, axis):
    count = lax.axis_size(axis)
    forward = [(i, (i + 1) % count) for i in range(count)]
    backward = [(target, source) for source, target in forward]
    return lax.ppermute(high, axis, forward), lax.ppermute(low, axis, backward)


def body(value, gust):
    rows_a, rows_b, rows_c, width = value.shape
    axes = ("ga", "gx", "gy")
    count_a = rows_a * lax.axis_size("ga")
    count_b = rows_b * lax.axis_size("gx")
    count_c = rows_c * lax.axis_size("gy")
    step_a = 2.0 * half_span / count_a
    step_b = 2.0 * half_span / count_b
    step_c = 2.0 * math.pi / count_c
    step_four = 1.0 / N4
    step_five = 1.0 / N5
    index_a = lax.axis_index("ga")
    index_b = lax.axis_index("gx")
    index_c = lax.axis_index("gy")

    low_c, high_c = exchange(value[:, :, :2], value[:, :, -2:], "gy")
    low_b, high_b = exchange(value[:, :2], value[:, -2:], "gx")
    low_a, high_a = exchange(value[:2], value[-2:], "ga")

    positions = lax.iota(jnp.int32, width)
    pos_one = -half_span + (
        (index_a * rows_a + lax.iota(jnp.int32, rows_a)).astype(jnp.float32) + 0.5
    ) * step_a
    pos_two = -half_span + (
        (index_b * rows_b + lax.iota(jnp.int32, rows_b)).astype(jnp.float32) + 0.5
    ) * step_b
    heading = (
        -math.pi + (index_c * rows_c + lax.iota(jnp.int32, rows_c)).astype(jnp.float32) * step_c
    ).reshape(rows_c, 1)
    speed_own = 0.5 + ((positions // (N5 * N6)).astype(jnp.float32) + 0.5) * step_four
    speed_other = 0.5 + ((positions // N6 % N5).astype(jnp.float32) + 0.5) * step_five
    turn_rate = ((positions % N6).astype(jnp.float32) - 0.5 * (N6 - 1)) * omega_step
    drift = jnp.stack(
        [speed_other * jnp.cos(heading) - speed_own, speed_other * jnp.sin(heading)]
    )
    rate = jnp.broadcast_to(turn_rate, (rows_c, width))
    flags = jnp.stack(
        [
            index_a == 0,
            index_a == lax.axis_size("ga") - 1,
            index_b == 0,
            index_b == lax.axis_size("gx") - 1,
        ]
    ).astype(jnp.float32)
    scal = jnp.concatenate([pos_one, pos_two, gust.reshape(-1), flags])

    full = jax.ShapeDtypeStruct(value.shape, jnp.float32)
    peaks = jax.ShapeDtypeStruct((3, 8, LANES), jnp.float32)

    lines = rows_a * rows_b
    flat = jax.ShapeDtypeStruct((lines, rows_c, width), jnp.float32)
    line = pl.BlockSpec((1, rows_c, width), lambda i: (i, 0, 0))
    g4, g5, g6, h_inner, most_inner = pl.pallas_call(
        inner_kernel,
        out_shape=(flat, flat, flat, flat, peaks),
        grid=(lines,),
        in_specs=[line, pl.BlockSpec((2, 4 * width // LANES, LANES), lambda i: (0, 0, 0))],
        out_specs=(line, line, line, line, pl.BlockSpec((3, 8, LANES), lambda i: (0, 0, 0))),
        cost_estimate=pl.CostEstimate(
            flops=60_000_000, bytes_accessed=10_000_000, transcendentals=4_000_000
        ),
        name="inner_axes",
    )(value.reshape(flat.shape), jnp.asarray(edge_codes()))
    g4, g5, g6, h_inner = [a.reshape(value.shape) for a in (g4, g5, g6, h_inner)]

    def block(*lead, lanes=1280):
        shape = (*lead, lanes)
        return pl.BlockSpec(shape, lambda i: (0,) * len(lead) + (i,))

    smem = pl.BlockSpec(memory_space=pltpu.SMEM)
    whole = block(4, 4, 4)
    turn = jnp.concatenate([low_c, high_c], axis=2)
    p1, m, h_part, g1, g3 = pl.pallas_call(
        lambda *refs: rows_kernel(step_a, step_c, *refs),
        out_shape=(full,) * 5,
        grid=(width // 1280,),
        in_specs=[smem, whole, block(2, 4, 4), block(2, 4, 4), whole, whole, block(2, 4), block(4)],
        out_specs=(whole,) * 5,
        cost_estimate=pl.CostEstimate(
            flops=40_000_000, bytes_accessed=16_000_000, transcendentals=2_000_000
        ),
        name="axes_1_and_3",
    )(scal, value, low_a, high_a, turn, h_inner, drift, rate)

    hamil, g2, most_outer = pl.pallas_call(
        lambda *refs: last_kernel(step_b, *refs),
        out_shape=(full, full, peaks),
        grid=(width // 1280,),
        in_specs=[smem, whole, block(4, 2, 4), block(4, 2, 4), whole, whole, whole, block(2, 4)],
        out_specs=(whole, whole, pl.BlockSpec((3, 8, LANES), lambda i: (0, 0, 0))),
        cost_estimate=pl.CostEstimate(
            flops=30_000_000, bytes_accessed=12_000_000, transcendentals=2_000_000
        ),
        name="axis_2_and_rates",
    )(scal, value, low_b, high_b, p1, m, h_part, drift)

    def saturate(x):
        return jnp.sqrt(x) * lax.rsqrt(x + soft)

    spin = jnp.abs(turn_rate[:LANES])
    inner = jnp.max(most_inner, axis=(1, 2))
    local = jnp.stack(
        [
            jnp.max(most_outer[0]),
            jnp.max(most_outer[1]),
            jnp.max(spin + turn_max * saturate(most_outer[2])),
            inner[0],
            inner[1],
            inner[2],
            inner[2],
            inner[2],
        ]
    )
    devices = lax.axis_size(axes)
    spread = lax.all_to_all(jnp.broadcast_to(local, (devices, 8)), axes, 0, 0, tiled=True)
    most = jnp.max(spread, axis=0)
    weights = jnp.array([accel_max, other_accel, spin_max], jnp.float32)
    speeds = jnp.concatenate([most[:3], weights * saturate(most[3:6])])
    spacing = jnp.array([step_a, step_b, step_c, step_four, step_five, omega_step], jnp.float32)
    per_step = speeds / spacing
    time_step = courant / jnp.sum(per_step)
    factors = (0.25 * time_step) * per_step
    total = factors[0] * g1
    for number, g in enumerate((g2, g3, g4, g5, g6)):
        total = total + factors[number + 1] * g
    value_next = value - time_step * hamil + total
    return (value_next, time_step.reshape(1))


def solution(mesh):
    in_specs = (P("ga", "gx", "gy", None), P("ga", "gx"))
    out_specs = (P("ga", "gx", "gy", None), P())
    return jax.shard_map(body, mesh=mesh, in_specs=in_specs, out_specs=out_specs, check_vma=False)
```

```python
import math

import jax
import jax.numpy as jnp
import numpy as np
from jax import lax
from jax.experimental import pallas as pl
from jax.experimental.pallas import tpu as pltpu
from jax.sharding import PartitionSpec as P

N4 = 40
N5 = 40
N6 = 4
WIDTH = N4 * N5 * N6
LANES = 128
PAIRS = WIDTH // (2 * LANES)

turn_max = 1.0
accel_max = 0.5
other_accel = 0.4
spin_max = 0.3
smooth_width = 0.25
courant = 0.5
weno_eps = 1e-06
omega_step = 0.05
half_span = 5.0
soft = smooth_width**2


def lanes(j, half):
    start = 256 * j + 128 * half
    return pl.ds(start if isinstance(j, int) else pl.multiple_of(start, 128), 128)


def load(ref, lead, j):
    return jnp.concatenate(
        [ref[(*lead, slice(None), lanes(j, half))] for half in range(2)], axis=0
    )


def store(ref, lead, j, x):
    ref[(*lead, slice(None), lanes(j, 0))] = x[:4]
    ref[(*lead, slice(None), lanes(j, 1))] = x[4:]


def wide(j):
    return pl.ds(pl.multiple_of(256 * j, 256), 256)


def rows(j):
    return pl.ds(8 * j if isinstance(j, int) else pl.multiple_of(8 * j, 8), 8)


def edge_kernel(v_ref, high_b_ref, sem):
    copy = pltpu.make_async_copy(v_ref.at[:, 2:4], high_b_ref, sem)
    copy.start()
    copy.wait()


def pack_kernel(v_ref, low_a_ref, high_a_ref, low_c_ref, high_c_ref):
    low_a_ref[...] = v_ref[0:2]
    high_a_ref[...] = v_ref[2:4]
    first = lax.broadcasted_iota(jnp.int32, (8, LANES), 0) % 4 < 2

    @pl.loop(0, 4)
    def _(b):
        for a in range(2):
            for j in range(PAIRS):
                near = load(v_ref, (a, b), j)
                far = load(v_ref, (a + 2, b), j)
                high_c_ref[a, b, rows(j), :] = jnp.where(first, pltpu.roll(near, 6, 0), far)
                low_c_ref[a, b, rows(j), :] = jnp.where(first, far, pltpu.roll(near, 2, 0))


def squared_curve(curve, eps):
    e = curve * curve + eps
    return e * e


def weno(d_back, d_here, s_back, s_here, s_ahead, q_back, q_here, q_ahead, scale):
    u_minus = (s_here - s_back) * (q_here / (q_here + (q_back + q_back)))
    u_plus = (s_ahead - s_here) * (q_here / (q_here + (q_ahead + q_ahead)))
    mean = scale * ((d_back + d_here) - 0.5 * (u_minus + u_plus))
    return mean, u_minus - u_plus


def column(values, spacing):
    eps = weno_eps * spacing**4
    d = [b - a for a, b in zip(values[:-1], values[1:])]
    s = [b - a for a, b in zip(d[:-1], d[1:])]
    q = [squared_curve(x, eps) for x in s]
    return [
        weno(d[i + 1], d[i + 2], s[i], s[i + 1], s[i + 2], q[i], q[i + 1], q[i + 2], 0.5 / spacing)
        for i in range(len(values) - 4)
    ]


def inner_kernel(v_ref, code_ref, g4_ref, g5_ref, g6_ref, h_ref, most_ref):
    lane = lax.broadcasted_iota(jnp.int32, (8, LANES), 1)
    upper = lax.broadcasted_iota(jnp.int32, (8, LANES), 0) < 4
    most_ref[...] = jnp.zeros_like(most_ref)

    def up4(r):
        y = [pltpu.roll(a, 4, 0) for a in r]
        return [jnp.where(upper, y[k], y[(k + 1) % PAIRS]) for k in range(PAIRS)]

    def down4(r):
        y = [pltpu.roll(a, 4, 0) for a in r]
        return [jnp.where(upper, y[k - 1], y[k]) for k in range(PAIRS)]

    def ahead(a, stride):
        n = stride % LANES
        r = [pltpu.roll(y, LANES - n, 1) for y in a]
        if stride == 1:
            return r
        u = up4(r)
        near, far = (r, u) if stride < LANES else (u, r[1:] + r[:1])
        return [jnp.where(lane < LANES - n, near[k], far[k]) for k in range(PAIRS)]

    def back(a, stride):
        n = stride % LANES
        r = [pltpu.roll(y, n, 1) for y in a]
        if stride == 1:
            return r
        u = down4(r)
        near, far = (r, u) if stride < LANES else (u, r[-1:] + r[:-1])
        return [jnp.where(lane >= n, near[k], far[k]) for k in range(PAIRS)]

    @pl.loop(0, 16)
    def _(line):
        lead = (lax.div(line, 4), lax.rem(line, 4))
        x = [load(v_ref, lead, j) for j in range(PAIRS)]
        total = [None] * PAIRS
        for stride, spacing, weight, g_ref, which in (
            (N5 * N6, 1.0 / N4, accel_max, g4_ref, 0),
            (N6, 1.0 / N5, -other_accel, g5_ref, 1),
            (1, omega_step, -spin_max, g6_ref, 2),
        ):
            eps = weno_eps * spacing**4
            if which < 2:
                codes = [code_ref[which, rows(k), :] for k in range(PAIRS)]
            else:
                place = lane % N6
                codes = [jnp.where(place == 0, -1, jnp.where(place == N6 - 1, 1, 0))] * PAIRS
            d = [b - a for a, b in zip(x, ahead(x, stride))]
            before = [a - b for a, b in zip(x, back(x, stride))]
            d_here = [jnp.where(c > 0, b, a) for c, a, b in zip(codes, d, before)]
            d_back = [jnp.where(c < 0, a, b) for c, a, b in zip(codes, d, before)]
            s = [a - b for a, b in zip(d_here, d_back)]
            s_ahead = ahead(s, stride)
            s_back = back(s, stride)
            peak = None
            for k in range(PAIRS):
                mean, diff = weno(
                    d_back[k],
                    d_here[k],
                    s_back[k],
                    s[k],
                    s_ahead[k],
                    squared_curve(s_back[k], eps),
                    squared_curve(s[k], eps),
                    squared_curve(s_ahead[k], eps),
                    0.5 / spacing,
                )
                store(g_ref, lead, k, diff)
                square = mean * mean
                peak = square if peak is None else jnp.maximum(peak, square)
                y = square + soft
                root = weight * (y * lax.rsqrt(y))
                total[k] = root if total[k] is None else total[k] + root
            most_ref[which] = jnp.maximum(most_ref[which], peak)
        for k in range(PAIRS):
            store(h_ref, lead, k, total[k])


def first_kernel(
    step_a, scal_ref, v_ref, low_ref, high_ref, _, __, p1_ref, g1_ref, low_b0_ref, low_b1_ref
):
    low_b0_ref[...] = v_ref[0:2, 0:2]
    low_b1_ref[...] = v_ref[2:4, 0:2]
    at_low = scal_ref[24] > 0.0
    at_high = scal_ref[25] > 0.0

    @pl.loop(0, PAIRS)
    def _(j):
        for b in range(4):
            v = [v_ref[a, b, :, wide(j)] for a in range(4)]
            low = [low_ref[a, b, :, wide(j)] for a in range(2)]
            high = [high_ref[a, b, :, wide(j)] for a in range(2)]
            low = [
                jnp.where(at_low, 3.0 * v[0] - 2.0 * v[1], low[0]),
                jnp.where(at_low, 2.0 * v[0] - v[1], low[1]),
            ]
            high = [
                jnp.where(at_high, 2.0 * v[3] - v[2], high[0]),
                jnp.where(at_high, 3.0 * v[3] - 2.0 * v[2], high[1]),
            ]
            for a, (p1, g1) in enumerate(column(low + v + high, step_a)):
                p1_ref[a, b, :, wide(j)] = p1
                g1_ref[a, b, :, wide(j)] = g1


def third_kernel(
    step_c, scal_ref, v_ref, before_ref, after_ref, h_ref, p1_ref, drift_ref, m_ref, hp_ref, g3_ref
):
    place = lax.broadcasted_iota(jnp.int32, (8, LANES), 0) % 4
    rate = (
        (lax.broadcasted_iota(jnp.int32, (8, LANES), 1) % N6).astype(jnp.float32)
        - 0.5 * (N6 - 1)
    ) * omega_step

    @pl.loop(0, PAIRS)
    def _(j):
        drift = load(drift_ref, (0,), j)
        for b in range(4):
            pos_two = scal_ref[4 + b]
            for a in range(4):
                x = load(v_ref, (a, b), j)
                before = before_ref[a % 2, b, rows(j), :]
                after = after_ref[a % 2, b, rows(j), :]
                if a >= 2:
                    before, after = pltpu.roll(before, 6, 0), pltpu.roll(after, 2, 0)
                ghost = jnp.where(place < 2, before, after)
                x_m2 = jnp.where(place < 2, ghost, pltpu.roll(x, 2, 0))
                x_m1 = jnp.where(place == 0, pltpu.roll(ghost, 7, 0), pltpu.roll(x, 1, 0))
                x_p1 = jnp.where(place == 3, pltpu.roll(ghost, 1, 0), pltpu.roll(x, 7, 0))
                x_p2 = jnp.where(place >= 2, ghost, pltpu.roll(x, 6, 0))
                (p3, g3), = column([x_m2, x_m1, x, x_p1, x_p2], step_c)
                p1 = load(p1_ref, (a, b), j)
                store(g3_ref, (a, b), j, g3)
                store(m_ref, (a, b), j, p1 * pos_two - p3)
                store(hp_ref, (a, b), j, p1 * drift + p3 * rate + load(h_ref, (a, b), j))


def saturate(x):
    return jnp.sqrt(x) * lax.rsqrt(x + soft)


def last_kernel(
    step_b, half, scal_ref, v_ref, low_ref, high_ref, p1_ref, m_ref, hp_ref, drift_ref, *refs
):
    *most_refs, h_ref, g2_ref, most_ref = refs
    at_low = scal_ref[26] > 0.0
    at_high = scal_ref[27] > 0.0

    def chunk(j, most):
        drift_one = drift_ref[0, :, wide(j)]
        drift_two = drift_ref[1, :, wide(j)]
        size_one = jnp.abs(drift_one)
        size_two = jnp.abs(drift_two)
        for k in range(2):
            a = 2 * half + k
            pos_one = scal_ref[a]
            v = [v_ref[a, b, :, wide(j)] for b in range(4)]
            low = [low_ref[a, b, :, wide(j)] for b in range(2)]
            high = [high_ref[k, b, :, wide(j)] for b in range(2)]
            low = [
                jnp.where(at_low, 3.0 * v[0] - 2.0 * v[1], low[0]),
                jnp.where(at_low, 2.0 * v[0] - v[1], low[1]),
            ]
            high = [
                jnp.where(at_high, 2.0 * v[3] - v[2], high[0]),
                jnp.where(at_high, 3.0 * v[3] - 2.0 * v[2], high[1]),
            ]
            for b, (p2, g2) in enumerate(column(low + v + high, step_b)):
                gust = scal_ref[8 + 4 * a + b]
                g2_ref[k, b, :, wide(j)] = g2
                p1 = p1_ref[a, b, :, wide(j)]
                switch = m_ref[a, b, :, wide(j)] - p2 * pos_one
                square = switch * switch
                y = square + soft
                r = lax.rsqrt(y)
                unit = jnp.abs(switch) * r
                push = (p1 * p1 + p2 * p2) + soft
                wind = gust * lax.rsqrt(push)
                one = size_one + unit * jnp.abs(scal_ref[4 + b]) + jnp.abs(p1) * wind
                two = size_two + unit * jnp.abs(pos_one) + jnp.abs(p2) * wind
                most = (
                    jnp.maximum(most[0], one),
                    jnp.maximum(most[1], two),
                    jnp.maximum(most[2], square),
                )
                hamil = hp_ref[a, b, :, wide(j)] + p2 * drift_two + y * r - wind * push
                h_ref[k, b, :, wide(j)] = hamil
        return most

    if half == 0:
        most = (jnp.zeros((4, 256), jnp.float32),) * 3
    else:
        most = tuple(most_refs[0][i] for i in range(3))
    most = list(lax.fori_loop(0, PAIRS, chunk, most))
    if half == 0:
        for i in range(3):
            most_ref[i] = most[i]
        return
    lane = lax.broadcasted_iota(jnp.int32, (4, 256), 1)
    spin = jnp.abs(((lane % N6).astype(jnp.float32) - 0.5 * (N6 - 1)) * omega_step)
    most[2] = spin + turn_max * saturate(most[2])
    most += [most_refs[1][i] for i in range(3)]
    row = jnp.zeros((1, LANES), jnp.float32)
    for i, x in enumerate(most):
        x = jnp.max(jnp.max(x, axis=0, keepdims=True), axis=1, keepdims=True)
        row = jnp.where(lane[:1, :LANES] == i, x, row)
    most_ref[...] = jnp.broadcast_to(row[None], most_ref.shape)


def update_kernel(
    spacings, v_ref, g1_ref, g3_ref, g4_ref, g5_ref, g6_ref, h0_ref, h1_ref, g20_ref, g21_ref,
    most_ref, o_ref, step_ref,
):
    most = jnp.max(most_ref[...], axis=0)
    lane = lax.broadcasted_iota(jnp.int32, (1, LANES), 1)
    weight = jnp.where(lane == 3, accel_max, jnp.where(lane == 4, other_accel, spin_max))
    speeds = jnp.where(lane < 3, most, weight * saturate(most))
    spacing = jnp.full((1, LANES), spacings[5], jnp.float32)
    for i in range(5):
        spacing = jnp.where(lane == i, spacings[i], spacing)
    per_step = jnp.where(lane < 6, speeds / spacing, 0.0)
    step = courant / jnp.sum(per_step, axis=1, keepdims=True)
    factors = [
        (0.25 * step) * jnp.sum(jnp.where(lane == i, per_step, 0.0), axis=1, keepdims=True)
        for i in range(6)
    ]
    step_ref[...] = step

    for half, h_ref, g2_ref in ((0, h0_ref, g20_ref), (1, h1_ref, g21_ref)):

        @pl.loop(0, 2)
        def _(k):
            for b in range(4):
                for j in range(5):
                    part = (b, slice(None), pl.ds(1280 * j, 1280))
                    at = (2 * half + k, *part)
                    total = v_ref[at] - step * h_ref[(k, *part)]
                    total = total + factors[0] * g1_ref[at]
                    total = total + factors[1] * g2_ref[(k, *part)]
                    for f, g_ref in zip(factors[2:], (g3_ref, g4_ref, g5_ref, g6_ref)):
                        total = total + f * g_ref[at]
                    o_ref[at] = total


def edge_codes():
    flat = np.arange(WIDTH).reshape(WIDTH // LANES, 1, LANES)
    flat = np.broadcast_to(flat, (WIDTH // LANES, 4, LANES)).reshape(-1, LANES)
    codes = []
    for stride, count in ((N5 * N6, N4), (N6, N5)):
        place = flat // stride % count
        codes.append(np.where(place == 0, -1, np.where(place == count - 1, 1, 0)))
    return np.stack(codes).astype(np.int32)


def forward(block, axis):
    count = lax.axis_size(axis)
    return lax.ppermute(block, axis, [(i, (i + 1) % count) for i in range(count)])


def backward(block, axis):
    count = lax.axis_size(axis)
    return lax.ppermute(block, axis, [((i + 1) % count, i) for i in range(count)])


def body(value, gust):
    rows_a, rows_b, rows_c, width = value.shape
    axes = ("ga", "gx", "gy")
    count_a = rows_a * lax.axis_size("ga")
    count_b = rows_b * lax.axis_size("gx")
    count_c = rows_c * lax.axis_size("gy")
    step_a = 2.0 * half_span / count_a
    step_b = 2.0 * half_span / count_b
    step_c = 2.0 * math.pi / count_c
    step_four = 1.0 / N4
    step_five = 1.0 / N5
    index_a = lax.axis_index("ga")
    index_b = lax.axis_index("gx")
    index_c = lax.axis_index("gy")

    vmem = pl.BlockSpec(memory_space=pltpu.VMEM)
    hbm = pl.BlockSpec(memory_space=pltpu.HBM)
    smem = pl.BlockSpec(memory_space=pltpu.SMEM)
    full = pltpu.VMEM(value.shape, jnp.float32)
    turn = pltpu.VMEM((2, 4, 4 * width // LANES, LANES), jnp.float32)

    def call(kernel, name, ins, outs, out_specs=None, scratch=()):
        return pl.pallas_call(
            kernel,
            name=name,
            out_shape=tuple(outs),
            in_specs=ins,
            out_specs=tuple(out_specs or [vmem] * len(outs)),
            scratch_shapes=scratch,
            compiler_params=pltpu.CompilerParams(vmem_limit_bytes=8 << 20),
            cost_estimate=pl.CostEstimate(flops=1, bytes_accessed=1, transcendentals=1),
        )

    slab_a = pltpu.VMEM((2, 4, 4, width), jnp.float32)
    slab_b = jax.ShapeDtypeStruct((4, 2, 4, width), jnp.float32)
    (send_high_b,) = call(
        edge_kernel,
        "edge",
        [hbm],
        [slab_b],
        out_specs=[hbm],
        scratch=[pltpu.SemaphoreType.DMA],
    )(value)
    low_b = forward(send_high_b, "gx")
    send_low_a, send_high_a, send_low_c, send_high_c = call(
        pack_kernel,
        "pack",
        [vmem],
        [slab_a, slab_a, turn, turn],
    )(value)
    low_c = forward(send_high_c, "gy")
    high_c = backward(send_low_c, "gy")
    low_a = forward(send_high_a, "ga")
    high_a = backward(send_low_a, "ga")

    positions = lax.iota(jnp.int32, width)
    pos_one = -half_span + (
        (index_a * rows_a + lax.iota(jnp.int32, rows_a)).astype(jnp.float32) + 0.5
    ) * step_a
    pos_two = -half_span + (
        (index_b * rows_b + lax.iota(jnp.int32, rows_b)).astype(jnp.float32) + 0.5
    ) * step_b
    heading = (
        -math.pi + (index_c * rows_c + lax.iota(jnp.int32, rows_c)).astype(jnp.float32) * step_c
    ).reshape(rows_c, 1)
    speed_own = 0.5 + ((positions // (N5 * N6)).astype(jnp.float32) + 0.5) * step_four
    speed_other = 0.5 + ((positions // N6 % N5).astype(jnp.float32) + 0.5) * step_five
    drift = jnp.stack(
        [speed_other * jnp.cos(heading) - speed_own, speed_other * jnp.sin(heading)]
    )
    flags = jnp.stack(
        [
            index_a == 0,
            index_a == lax.axis_size("ga") - 1,
            index_b == 0,
            index_b == lax.axis_size("gx") - 1,
        ]
    ).astype(jnp.float32)
    scal = jnp.concatenate([pos_one, pos_two, gust.reshape(-1), flags])

    g4, g5, g6, h_inner, most_inner = call(
        inner_kernel,
        "inner_axes",
        [vmem] * 2,
        [full] * 4 + [pltpu.VMEM((3, 8, LANES), jnp.float32)],
    )(value, jnp.asarray(edge_codes()))
    slab_b = jax.ShapeDtypeStruct((2, 2, 4, width), jnp.float32)
    p1, g1, *send_low_b = call(
        lambda *refs: first_kernel(step_a, *refs),
        "axis_1",
        [smem] + [vmem] * 3 + [hbm, vmem],
        [full, full, slab_b, slab_b],
    )(scal, value, low_a, high_a, low_b, most_inner)
    high_b = [backward(x, "gx") for x in send_low_b]

    m, h_part, g3 = call(
        lambda *refs: third_kernel(step_c, *refs),
        "axis_3",
        [smem] + [vmem] * 6,
        [full] * 3,
    )(scal, value, low_c, high_c, h_inner, p1, drift)

    devices = lax.axis_size(axes)
    part = pltpu.VMEM((2, *value.shape[1:]), jnp.float32)
    inputs = (p1, m, h_part, drift)
    h0, g20, most = call(
        lambda *refs: last_kernel(step_b, 0, *refs),
        "axis_2_and_rates_0",
        [smem] + [vmem] * 7,
        [part, part, pltpu.VMEM((3, 4, 256), jnp.float32)],
    )(scal, value, low_b, high_b[0], *inputs)
    h1, g21, local = call(
        lambda *refs: last_kernel(step_b, 1, *refs),
        "axis_2_and_rates_1",
        [smem] + [vmem] * 9,
        [part, part, pltpu.VMEM((devices, 1, LANES), jnp.float32)],
    )(scal, value, low_b, high_b[1], *inputs, most, most_inner)

    spread = lax.all_to_all(local, axes, 0, 0, tiled=True)
    spacings = (step_a, step_b, step_c, step_four, step_five, omega_step)
    value_next, time_step = call(
        lambda *refs: update_kernel(spacings, *refs),
        "update",
        [vmem] * 11,
        [jax.ShapeDtypeStruct(value.shape, jnp.float32), jax.ShapeDtypeStruct((1, 1), jnp.float32)],
    )(value, g1, g3, g4, g5, g6, h0, h1, g20, g21, spread)
    return (value_next, time_step.reshape(1))


def solution(mesh):
    in_specs = (P("ga", "gx", "gy", None), P("ga", "gx"))
    out_specs = (P("ga", "gx", "gy", None), P())
    return jax.shard_map(body, mesh=mesh, in_specs=in_specs, out_specs=out_specs, check_vma=False)
```

```python
import math

import jax
import jax.numpy as jnp
import numpy as np
from jax import lax
from jax.experimental import pallas as pl
from jax.experimental.pallas import tpu as pltpu
from jax.sharding import PartitionSpec as P

N4 = 40
N5 = 40
N6 = 4
WIDTH = N4 * N5 * N6
LANES = 128
PAIRS = WIDTH // (2 * LANES)

turn_max = 1.0
accel_max = 0.5
other_accel = 0.4
spin_max = 0.3
smooth_width = 0.25
courant = 0.5
weno_eps = 1e-06
omega_step = 0.05
half_span = 5.0
soft = smooth_width**2


def lanes(j, half):
    start = 256 * j + 128 * half
    return pl.ds(start if isinstance(j, int) else pl.multiple_of(start, 128), 128)


def load(ref, lead, j):
    return jnp.concatenate(
        [ref[(*lead, slice(None), lanes(j, half))] for half in range(2)], axis=0
    )


def store(ref, lead, j, x):
    ref[(*lead, slice(None), lanes(j, 0))] = x[:4]
    ref[(*lead, slice(None), lanes(j, 1))] = x[4:]


def wide(j):
    return pl.ds(pl.multiple_of(256 * j, 256), 256)


def rows(j):
    return pl.ds(8 * j if isinstance(j, int) else pl.multiple_of(8 * j, 8), 8)


def pack_kernel(src_ref, _, v_ref, low_a_ref, high_a_ref, low_c_ref, high_c_ref, sem):
    copy = pltpu.make_async_copy(src_ref, v_ref, sem)
    copy.start()
    copy.wait()
    low_a_ref[...] = v_ref[0:2]
    high_a_ref[...] = v_ref[2:4]
    first = lax.broadcasted_iota(jnp.int32, (8, LANES), 0) % 4 < 2

    @pl.loop(0, 4)
    def _(b):
        for a in range(2):
            for j in range(PAIRS):
                near = load(v_ref, (a, b), j)
                far = load(v_ref, (a + 2, b), j)
                high_c_ref[a, b, rows(j), :] = jnp.where(first, pltpu.roll(near, 6, 0), far)
                low_c_ref[a, b, rows(j), :] = jnp.where(first, far, pltpu.roll(near, 2, 0))


def squared_curve(curve, eps):
    e = curve * curve + eps
    return e * e


def weno(d_back, d_here, s_back, s_here, s_ahead, q_back, q_here, q_ahead, scale):
    u_minus = (s_here - s_back) * (q_here / (q_here + (q_back + q_back)))
    u_plus = (s_ahead - s_here) * (q_here / (q_here + (q_ahead + q_ahead)))
    mean = scale * ((d_back + d_here) - 0.5 * (u_minus + u_plus))
    return mean, u_minus - u_plus


def column(values, spacing):
    eps = weno_eps * spacing**4
    d = [b - a for a, b in zip(values[:-1], values[1:])]
    s = [b - a for a, b in zip(d[:-1], d[1:])]
    q = [squared_curve(x, eps) for x in s]
    return [
        weno(d[i + 1], d[i + 2], s[i], s[i + 1], s[i + 2], q[i], q[i + 1], q[i + 2], 0.5 / spacing)
        for i in range(len(values) - 4)
    ]


def inner_kernel(v_ref, code_ref, g4_ref, g5_ref, g6_ref, h_ref, most_ref):
    lane = lax.broadcasted_iota(jnp.int32, (8, LANES), 1)
    upper = lax.broadcasted_iota(jnp.int32, (8, LANES), 0) < 4
    most_ref[...] = jnp.zeros_like(most_ref)

    def up4(r):
        y = [pltpu.roll(a, 4, 0) for a in r]
        return [jnp.where(upper, y[k], y[(k + 1) % PAIRS]) for k in range(PAIRS)]

    def down4(r):
        y = [pltpu.roll(a, 4, 0) for a in r]
        return [jnp.where(upper, y[k - 1], y[k]) for k in range(PAIRS)]

    def ahead(a, stride):
        n = stride % LANES
        r = [pltpu.roll(y, LANES - n, 1) for y in a]
        if stride == 1:
            return r
        u = up4(r)
        near, far = (r, u) if stride < LANES else (u, r[1:] + r[:1])
        return [jnp.where(lane < LANES - n, near[k], far[k]) for k in range(PAIRS)]

    def back(a, stride):
        n = stride % LANES
        r = [pltpu.roll(y, n, 1) for y in a]
        if stride == 1:
            return r
        u = down4(r)
        near, far = (r, u) if stride < LANES else (u, r[-1:] + r[:-1])
        return [jnp.where(lane >= n, near[k], far[k]) for k in range(PAIRS)]

    @pl.loop(0, 16)
    def _(line):
        lead = (lax.div(line, 4), lax.rem(line, 4))
        x = [load(v_ref, lead, j) for j in range(PAIRS)]
        total = [None] * PAIRS
        for stride, spacing, weight, g_ref, which in (
            (N5 * N6, 1.0 / N4, accel_max, g4_ref, 0),
            (N6, 1.0 / N5, -other_accel, g5_ref, 1),
            (1, omega_step, -spin_max, g6_ref, 2),
        ):
            eps = weno_eps * spacing**4
            if which < 2:
                codes = [code_ref[which, rows(k), :] for k in range(PAIRS)]
            else:
                place = lane % N6
                codes = [jnp.where(place == 0, -1, jnp.where(place == N6 - 1, 1, 0))] * PAIRS
            d = [b - a for a, b in zip(x, ahead(x, stride))]
            before = [a - b for a, b in zip(x, back(x, stride))]
            d_here = [jnp.where(c > 0, b, a) for c, a, b in zip(codes, d, before)]
            d_back = [jnp.where(c < 0, a, b) for c, a, b in zip(codes, d, before)]
            s = [a - b for a, b in zip(d_here, d_back)]
            s_ahead = ahead(s, stride)
            s_back = back(s, stride)
            peak = None
            for k in range(PAIRS):
                mean, diff = weno(
                    d_back[k],
                    d_here[k],
                    s_back[k],
                    s[k],
                    s_ahead[k],
                    squared_curve(s_back[k], eps),
                    squared_curve(s[k], eps),
                    squared_curve(s_ahead[k], eps),
                    0.5 / spacing,
                )
                store(g_ref, lead, k, diff)
                square = mean * mean
                peak = square if peak is None else jnp.maximum(peak, square)
                y = square + soft
                root = weight * (y * lax.rsqrt(y))
                total[k] = root if total[k] is None else total[k] + root
            most_ref[which] = jnp.maximum(most_ref[which], peak)
        for k in range(PAIRS):
            store(h_ref, lead, k, total[k])


def send_kernel(v_ref, *refs):
    low_b0_ref, low_b1_ref = refs[-2:]
    low_b0_ref[...] = v_ref[0:2, 0:2]
    low_b1_ref[...] = v_ref[2:4, 0:2]


def first_kernel(step_a, scal_ref, v_ref, low_ref, high_ref, p1_ref, g1_ref):
    at_low = scal_ref[24] > 0.0
    at_high = scal_ref[25] > 0.0

    @pl.loop(0, PAIRS)
    def _(j):
        for b in range(4):
            v = [v_ref[a, b, :, wide(j)] for a in range(4)]
            low = [low_ref[a, b, :, wide(j)] for a in range(2)]
            high = [high_ref[a, b, :, wide(j)] for a in range(2)]
            low = [
                jnp.where(at_low, 3.0 * v[0] - 2.0 * v[1], low[0]),
                jnp.where(at_low, 2.0 * v[0] - v[1], low[1]),
            ]
            high = [
                jnp.where(at_high, 2.0 * v[3] - v[2], high[0]),
                jnp.where(at_high, 3.0 * v[3] - 2.0 * v[2], high[1]),
            ]
            for a, (p1, g1) in enumerate(column(low + v + high, step_a)):
                p1_ref[a, b, :, wide(j)] = p1
                g1_ref[a, b, :, wide(j)] = g1


def third_kernel(
    step_c, scal_ref, v_ref, before_ref, after_ref, h_ref, p1_ref, drift_ref,
    m_ref, hp_ref, size_ref, square_ref, g3_ref,
):
    place = lax.broadcasted_iota(jnp.int32, (8, LANES), 0) % 4
    rate = (
        (lax.broadcasted_iota(jnp.int32, (8, LANES), 1) % N6).astype(jnp.float32)
        - 0.5 * (N6 - 1)
    ) * omega_step

    @pl.loop(0, PAIRS)
    def _(j):
        drift = load(drift_ref, (0,), j)
        for b in range(4):
            pos_two = scal_ref[4 + b]
            for a in range(4):
                x = load(v_ref, (a, b), j)
                before = before_ref[a % 2, b, rows(j), :]
                after = after_ref[a % 2, b, rows(j), :]
                if a >= 2:
                    before, after = pltpu.roll(before, 6, 0), pltpu.roll(after, 2, 0)
                ghost = jnp.where(place < 2, before, after)
                x_m2 = jnp.where(place < 2, ghost, pltpu.roll(x, 2, 0))
                x_m1 = jnp.where(place == 0, pltpu.roll(ghost, 7, 0), pltpu.roll(x, 1, 0))
                x_p1 = jnp.where(place == 3, pltpu.roll(ghost, 1, 0), pltpu.roll(x, 7, 0))
                x_p2 = jnp.where(place >= 2, ghost, pltpu.roll(x, 6, 0))
                (p3, g3), = column([x_m2, x_m1, x, x_p1, x_p2], step_c)
                p1 = load(p1_ref, (a, b), j)
                store(g3_ref, (a, b), j, g3)
                store(size_ref, (a, b), j, jnp.abs(p1))
                store(square_ref, (a, b), j, p1 * p1 + soft)
                store(m_ref, (a, b), j, p1 * pos_two - p3)
                store(hp_ref, (a, b), j, p1 * drift + p3 * rate + load(h_ref, (a, b), j))


def saturate(x):
    return jnp.sqrt(x) * lax.rsqrt(x + soft)


def last_kernel(
    step_b, lines, upper, final, scal_ref, v_ref, ghost_ref, size_ref, square_ref, m_ref, hp_ref,
    drift_ref, *refs,
):
    *most_refs, h_ref, g2_ref, most_ref = refs
    at_edge = scal_ref[27 if upper else 26] > 0.0

    def chunk(j, most):
        drift_one = drift_ref[0, :, wide(j)]
        drift_two = drift_ref[1, :, wide(j)]
        size_one = jnp.abs(drift_one)
        size_two = jnp.abs(drift_two)
        for k, a in enumerate(lines):
            pos_one = scal_ref[a]
            v = [v_ref[a, b, :, wide(j)] for b in range(4)]
            ghost = [ghost_ref[a if ghost_ref.shape[0] == 4 else k, b, :, wide(j)] for b in range(2)]
            if upper:
                v += [
                    jnp.where(at_edge, 2.0 * v[3] - v[2], ghost[0]),
                    jnp.where(at_edge, 3.0 * v[3] - 2.0 * v[2], ghost[1]),
                ]
            else:
                v = [
                    jnp.where(at_edge, 3.0 * v[0] - 2.0 * v[1], ghost[0]),
                    jnp.where(at_edge, 2.0 * v[0] - v[1], ghost[1]),
                ] + v
            for i, (p2, g2) in enumerate(column(v, step_b)):
                b = i + 2 if upper else i
                gust = scal_ref[8 + 4 * a + b]
                g2_ref[k, i, :, wide(j)] = g2
                switch = m_ref[a, b, :, wide(j)] - p2 * pos_one
                square = switch * switch
                y = square + soft
                r = lax.rsqrt(y)
                unit = jnp.abs(switch) * r
                push = square_ref[a, b, :, wide(j)] + p2 * p2
                wind = gust * lax.rsqrt(push)
                one = size_one + unit * jnp.abs(scal_ref[4 + b]) + size_ref[a, b, :, wide(j)] * wind
                two = size_two + unit * jnp.abs(pos_one) + jnp.abs(p2) * wind
                most = (
                    jnp.maximum(most[0], one),
                    jnp.maximum(most[1], two),
                    jnp.maximum(most[2], square),
                )
                hamil = hp_ref[a, b, :, wide(j)] + p2 * drift_two + y * r - wind * push
                h_ref[k, i, :, wide(j)] = hamil
        return most

    if most_refs:
        most = tuple(most_refs[0][i] for i in range(3))
    else:
        most = (jnp.zeros((4, 256), jnp.float32),) * 3
    most = list(lax.fori_loop(0, PAIRS, chunk, most, unroll=5))
    if not final:
        for i in range(3):
            most_ref[i] = most[i]
        return
    lane = lax.broadcasted_iota(jnp.int32, (4, 256), 1)
    spin = jnp.abs(((lane % N6).astype(jnp.float32) - 0.5 * (N6 - 1)) * omega_step)
    most[2] = spin + turn_max * saturate(most[2])
    most += [most_refs[1][i] for i in range(3)]
    row = jnp.zeros((1, LANES), jnp.float32)
    for i, x in enumerate(most):
        x = jnp.max(jnp.max(x, axis=0, keepdims=True), axis=1, keepdims=True)
        row = jnp.where(lane[:1, :LANES] == i, x, row)
    most_ref[...] = jnp.broadcast_to(row, most_ref.shape)


def update_kernel(
    spacings, v_ref, g1_ref, g3_ref, g4_ref, g5_ref, g6_ref, h0_ref, h1_ref, h2_ref,
    g20_ref, g21_ref, g22_ref, most_ref, o_ref, step_ref,
):
    most = jnp.max(most_ref[...], axis=0, keepdims=True)
    lane = lax.broadcasted_iota(jnp.int32, (1, LANES), 1)
    weight = jnp.where(lane == 3, accel_max, jnp.where(lane == 4, other_accel, spin_max))
    speeds = jnp.where(lane < 3, most, weight * saturate(most))
    spacing = jnp.full((1, LANES), spacings[5], jnp.float32)
    for i in range(5):
        spacing = jnp.where(lane == i, spacings[i], spacing)
    per_step = jnp.where(lane < 6, speeds / spacing, 0.0)
    step = courant / jnp.sum(per_step, axis=1, keepdims=True)
    factors = [
        (0.25 * step) * jnp.sum(jnp.where(lane == i, per_step, 0.0), axis=1, keepdims=True)
        for i in range(6)
    ]
    step_ref[...] = step

    for half, h_high, g2_high in ((0, h1_ref, g21_ref), (1, h2_ref, g22_ref)):

        @pl.loop(0, 2)
        def _(k):
            a = 2 * half + k
            for b in range(4):
                for j in range(5):
                    at = (a, b, slice(None), pl.ds(1280 * j, 1280))
                    near = (k, b - 2, slice(None), pl.ds(1280 * j, 1280))
                    h = h0_ref[at] if b < 2 else h_high[near]
                    g2 = g20_ref[at] if b < 2 else g2_high[near]
                    total = v_ref[at] - step * h
                    total = total + factors[0] * g1_ref[at]
                    total = total + factors[1] * g2
                    for f, g_ref in zip(factors[2:], (g3_ref, g4_ref, g5_ref, g6_ref)):
                        total = total + f * g_ref[at]
                    o_ref[at] = total


def edge_codes():
    flat = np.arange(WIDTH).reshape(WIDTH // LANES, 1, LANES)
    flat = np.broadcast_to(flat, (WIDTH // LANES, 4, LANES)).reshape(-1, LANES)
    codes = []
    for stride, count in ((N5 * N6, N4), (N6, N5)):
        place = flat // stride % count
        codes.append(np.where(place == 0, -1, np.where(place == count - 1, 1, 0)))
    return np.stack(codes).astype(np.int32)


def forward(block, axis):
    count = lax.axis_size(axis)
    return lax.ppermute(block, axis, [(i, (i + 1) % count) for i in range(count)])


def backward(block, axis):
    count = lax.axis_size(axis)
    return lax.ppermute(block, axis, [((i + 1) % count, i) for i in range(count)])


def body(value, gust):
    rows_a, rows_b, rows_c, width = value.shape
    axes = ("ga", "gx", "gy")
    count_a = rows_a * lax.axis_size("ga")
    count_b = rows_b * lax.axis_size("gx")
    count_c = rows_c * lax.axis_size("gy")
    step_a = 2.0 * half_span / count_a
    step_b = 2.0 * half_span / count_b
    step_c = 2.0 * math.pi / count_c
    step_four = 1.0 / N4
    step_five = 1.0 / N5
    index_a = lax.axis_index("ga")
    index_b = lax.axis_index("gx")
    index_c = lax.axis_index("gy")

    vmem = pl.BlockSpec(memory_space=pltpu.VMEM)
    hbm = pl.BlockSpec(memory_space=pltpu.HBM)
    smem = pl.BlockSpec(memory_space=pltpu.SMEM)
    full = pltpu.VMEM(value.shape, jnp.float32)
    turn = pltpu.VMEM((2, 4, 4 * width // LANES, LANES), jnp.float32)

    def call(kernel, name, ins, outs, out_specs=None, scratch=()):
        return pl.pallas_call(
            kernel,
            name=name,
            out_shape=tuple(outs),
            in_specs=ins,
            out_specs=tuple(out_specs or [vmem] * len(outs)),
            scratch_shapes=scratch,
            compiler_params=pltpu.CompilerParams(vmem_limit_bytes=8 << 20),
            cost_estimate=pl.CostEstimate(flops=1, bytes_accessed=1, transcendentals=1),
        )

    slab_a = pltpu.VMEM((2, 4, 4, width), jnp.float32)
    slab_b = pltpu.VMEM((4, 2, 4, width), jnp.float32)
    send_high_b = value[:, 2:4]
    low_b = forward(send_high_b, "gx")
    value, send_low_a, send_high_a, send_low_c, send_high_c = call(
        pack_kernel,
        "pack",
        [hbm, hbm],
        [full, slab_a, slab_a, turn, turn],
        scratch=[pltpu.SemaphoreType.DMA],
    )(pltpu.with_memory_space_constraint(value, pltpu.HBM), send_high_b)
    low_c = forward(send_high_c, "gy")
    high_c = backward(send_low_c, "gy")
    low_a = forward(send_high_a, "ga")
    high_a = backward(send_low_a, "ga")

    positions = lax.iota(jnp.int32, width)
    pos_one = -half_span + (
        (index_a * rows_a + lax.iota(jnp.int32, rows_a)).astype(jnp.float32) + 0.5
    ) * step_a
    pos_two = -half_span + (
        (index_b * rows_b + lax.iota(jnp.int32, rows_b)).astype(jnp.float32) + 0.5
    ) * step_b
    heading = (
        -math.pi + (index_c * rows_c + lax.iota(jnp.int32, rows_c)).astype(jnp.float32) * step_c
    ).reshape(rows_c, 1)
    speed_own = 0.5 + ((positions // (N5 * N6)).astype(jnp.float32) + 0.5) * step_four
    speed_other = 0.5 + ((positions // N6 % N5).astype(jnp.float32) + 0.5) * step_five
    drift = jnp.stack(
        [speed_other * jnp.cos(heading) - speed_own, speed_other * jnp.sin(heading)]
    )
    flags = jnp.stack(
        [
            index_a == 0,
            index_a == lax.axis_size("ga") - 1,
            index_b == 0,
            index_b == lax.axis_size("gx") - 1,
        ]
    ).astype(jnp.float32)
    scal = jnp.concatenate([pos_one, pos_two, gust.reshape(-1), flags])

    g4, g5, g6, h_inner, most_inner = call(
        inner_kernel,
        "inner_axes",
        [vmem] * 2,
        [full] * 4 + [pltpu.VMEM((3, 8, LANES), jnp.float32)],
    )(value, jnp.asarray(edge_codes()))
    slab_b = jax.ShapeDtypeStruct((2, 2, 4, width), jnp.float32)
    send_low_b = call(
        send_kernel,
        "send",
        [vmem] + [hbm] * 4,
        [slab_b, slab_b],
    )(value, low_a, high_a, low_b, most_inner)
    high_b = [backward(x, "gx") for x in send_low_b]

    p1, g1 = call(
        lambda *refs: first_kernel(step_a, *refs),
        "axis_1",
        [smem] + [vmem] * 3,
        [full, full],
    )(scal, value, low_a, high_a)

    m, h_part, size, square, g3 = call(
        lambda *refs: third_kernel(step_c, *refs),
        "axis_3",
        [smem] + [vmem] * 6,
        [full] * 5,
    )(scal, value, low_c, high_c, h_inner, p1, drift)

    devices = lax.axis_size(axes)
    inputs = (size, square, m, h_part, drift)

    def last(name, lines, upper, ghost, *most):
        part = pltpu.VMEM((len(lines), 2, *value.shape[2:]), jnp.float32)
        final = len(most) > 1
        peaks = (devices, LANES) if final else (3, 4, 256)
        return call(
            lambda *refs: last_kernel(step_b, lines, upper, final, *refs),
            name,
            [smem] + [vmem] * (7 + len(most)),
            [part, part, pltpu.VMEM(peaks, jnp.float32)],
        )(scal, value, ghost, *inputs, *most)

    h0, g20, most = last("rates_0", (0, 1, 2, 3), False, low_b)
    h1, g21, most = last("rates_1", (0, 1), True, high_b[0], most)
    h2, g22, local = last("rates_2", (2, 3), True, high_b[1], most, most_inner)

    spread = lax.all_to_all(local, axes, 0, 0, tiled=True)
    spacings = (step_a, step_b, step_c, step_four, step_five, omega_step)
    value_next, time_step = call(
        lambda *refs: update_kernel(spacings, *refs),
        "update",
        [vmem] * 13,
        [jax.ShapeDtypeStruct(value.shape, jnp.float32), jax.ShapeDtypeStruct((1, 1), jnp.float32)],
    )(value, g1, g3, g4, g5, g6, h0, h1, h2, g20, g21, g22, spread)
    return (value_next, time_step.reshape(1))


def solution(mesh):
    in_specs = (P("ga", "gx", "gy", None), P("ga", "gx"))
    out_specs = (P("ga", "gx", "gy", None), P())
    return jax.shard_map(body, mesh=mesh, in_specs=in_specs, out_specs=out_specs, check_vma=False)
```

```python
import math

import jax
import jax.numpy as jnp
import numpy as np
from jax import lax
from jax.experimental import pallas as pl
from jax.experimental.pallas import tpu as pltpu
from jax.sharding import PartitionSpec as P

N4 = 40
N5 = 40
N6 = 4
WIDTH = N4 * N5 * N6
LANES = 128
PAIRS = WIDTH // (2 * LANES)

turn_max = 1.0
accel_max = 0.5
other_accel = 0.4
spin_max = 0.3
smooth_width = 0.25
courant = 0.5
weno_eps = 1e-06
omega_step = 0.05
half_span = 5.0
soft = smooth_width**2


def lanes(j, half):
    start = 256 * j + 128 * half
    return pl.ds(start if isinstance(j, int) else pl.multiple_of(start, 128), 128)


def load(ref, lead, j):
    return jnp.concatenate(
        [ref[(*lead, slice(None), lanes(j, half))] for half in range(2)], axis=0
    )


def store(ref, lead, j, x):
    ref[(*lead, slice(None), lanes(j, 0))] = x[:4]
    ref[(*lead, slice(None), lanes(j, 1))] = x[4:]


def wide(j):
    return pl.ds(pl.multiple_of(256 * j, 256), 256)


def rows(j):
    return pl.ds(8 * j if isinstance(j, int) else pl.multiple_of(8 * j, 8), 8)


def pack_kernel(src_ref, _, v_ref, low_a_ref, high_a_ref, low_c_ref, high_c_ref, sem):
    copy = pltpu.make_async_copy(src_ref, v_ref, sem)
    copy.start()
    copy.wait()
    low_a_ref[...] = v_ref[0:2]
    high_a_ref[...] = v_ref[2:4]
    first = lax.broadcasted_iota(jnp.int32, (8, LANES), 0) % 4 < 2

    @pl.loop(0, 4)
    def _(b):
        for a in range(2):
            for j in range(PAIRS):
                near = load(v_ref, (a, b), j)
                far = load(v_ref, (a + 2, b), j)
                high_c_ref[a, b, rows(j), :] = jnp.where(first, pltpu.roll(near, 6, 0), far)
                low_c_ref[a, b, rows(j), :] = jnp.where(first, far, pltpu.roll(near, 2, 0))


def squared_curve(curve, eps):
    e = curve * curve + eps
    return e * e


def weno(d_back, d_here, s_back, s_here, s_ahead, q_back, q_here, q_ahead, scale):
    u_minus = (s_here - s_back) * (q_here / (q_here + (q_back + q_back)))
    u_plus = (s_ahead - s_here) * (q_here / (q_here + (q_ahead + q_ahead)))
    mean = scale * ((d_back + d_here) - 0.5 * (u_minus + u_plus))
    return mean, u_minus - u_plus


def column(values, spacing):
    eps = weno_eps * spacing**4
    d = [b - a for a, b in zip(values[:-1], values[1:])]
    s = [b - a for a, b in zip(d[:-1], d[1:])]
    q = [squared_curve(x, eps) for x in s]
    return [
        weno(d[i + 1], d[i + 2], s[i], s[i + 1], s[i + 2], q[i], q[i + 1], q[i + 2], 0.5 / spacing)
        for i in range(len(values) - 4)
    ]


def inner_kernel(v_ref, code_ref, g4_ref, g5_ref, g6_ref, h_ref, most_ref):
    lane = lax.broadcasted_iota(jnp.int32, (8, LANES), 1)
    upper = lax.broadcasted_iota(jnp.int32, (8, LANES), 0) < 4
    most_ref[...] = jnp.zeros_like(most_ref)

    def up4(r):
        y = [pltpu.roll(a, 4, 0) for a in r]
        return [jnp.where(upper, y[k], y[(k + 1) % PAIRS]) for k in range(PAIRS)]

    def down4(r):
        y = [pltpu.roll(a, 4, 0) for a in r]
        return [jnp.where(upper, y[k - 1], y[k]) for k in range(PAIRS)]

    def ahead(a, stride):
        n = stride % LANES
        r = [pltpu.roll(y, LANES - n, 1) for y in a]
        if stride == 1:
            return r
        u = up4(r)
        near, far = (r, u) if stride < LANES else (u, r[1:] + r[:1])
        return [jnp.where(lane < LANES - n, near[k], far[k]) for k in range(PAIRS)]

    def back(a, stride):
        n = stride % LANES
        r = [pltpu.roll(y, n, 1) for y in a]
        if stride == 1:
            return r
        u = down4(r)
        near, far = (r, u) if stride < LANES else (u, r[-1:] + r[:-1])
        return [jnp.where(lane >= n, near[k], far[k]) for k in range(PAIRS)]

    @pl.loop(0, 16)
    def _(line):
        lead = (lax.div(line, 4), lax.rem(line, 4))
        x = [load(v_ref, lead, j) for j in range(PAIRS)]
        total = [None] * PAIRS
        for stride, spacing, weight, g_ref, which in (
            (N5 * N6, 1.0 / N4, accel_max, g4_ref, 0),
            (N6, 1.0 / N5, -other_accel, g5_ref, 1),
            (1, omega_step, -spin_max, g6_ref, 2),
        ):
            eps = weno_eps * spacing**4
            if which < 2:
                codes = [code_ref[which, rows(k), :] for k in range(PAIRS)]
            else:
                place = lane % N6
                codes = [jnp.where(place == 0, -1, jnp.where(place == N6 - 1, 1, 0))] * PAIRS
            d = [b - a for a, b in zip(x, ahead(x, stride))]
            before = [a - b for a, b in zip(x, back(x, stride))]
            d_here = [jnp.where(c > 0, b, a) for c, a, b in zip(codes, d, before)]
            d_back = [jnp.where(c < 0, a, b) for c, a, b in zip(codes, d, before)]
            s = [a - b for a, b in zip(d_here, d_back)]
            s_ahead = ahead(s, stride)
            s_back = back(s, stride)
            peak = None
            for k in range(PAIRS):
                mean, diff = weno(
                    d_back[k],
                    d_here[k],
                    s_back[k],
                    s[k],
                    s_ahead[k],
                    squared_curve(s_back[k], eps),
                    squared_curve(s[k], eps),
                    squared_curve(s_ahead[k], eps),
                    0.5 / spacing,
                )
                store(g_ref, lead, k, diff)
                square = mean * mean
                peak = square if peak is None else jnp.maximum(peak, square)
                y = square + soft
                root = weight * (y * lax.rsqrt(y))
                total[k] = root if total[k] is None else total[k] + root
            most_ref[which] = jnp.maximum(most_ref[which], peak)
        for k in range(PAIRS):
            store(h_ref, lead, k, total[k])


def send_kernel(v_ref, *refs):
    low_b0_ref, low_b1_ref = refs[-2:]
    low_b0_ref[...] = v_ref[0:2, 0:2]
    low_b1_ref[...] = v_ref[2:4, 0:2]


def first_kernel(step_a, scal_ref, v_ref, low_ref, high_ref, p1_ref, g1_ref):
    at_low = scal_ref[24] > 0.0
    at_high = scal_ref[25] > 0.0

    @pl.loop(0, PAIRS)
    def _(j):
        for b in range(4):
            v = [v_ref[a, b, :, wide(j)] for a in range(4)]
            low = [low_ref[a, b, :, wide(j)] for a in range(2)]
            high = [high_ref[a, b, :, wide(j)] for a in range(2)]
            low = [
                jnp.where(at_low, 3.0 * v[0] - 2.0 * v[1], low[0]),
                jnp.where(at_low, 2.0 * v[0] - v[1], low[1]),
            ]
            high = [
                jnp.where(at_high, 2.0 * v[3] - v[2], high[0]),
                jnp.where(at_high, 3.0 * v[3] - 2.0 * v[2], high[1]),
            ]
            for a, (p1, g1) in enumerate(column(low + v + high, step_a)):
                p1_ref[a, b, :, wide(j)] = p1
                g1_ref[a, b, :, wide(j)] = g1


def third_kernel(
    step_c, scal_ref, v_ref, before_ref, after_ref, h_ref, p1_ref, drift_ref,
    m_ref, hp_ref, g3_ref,
):
    place = lax.broadcasted_iota(jnp.int32, (8, LANES), 0) % 4
    rate = (
        (lax.broadcasted_iota(jnp.int32, (8, LANES), 1) % N6).astype(jnp.float32)
        - 0.5 * (N6 - 1)
    ) * omega_step

    @pl.loop(0, PAIRS)
    def _(j):
        drift = load(drift_ref, (0,), j)
        for b in range(4):
            pos_two = scal_ref[4 + b]
            for a in range(4):
                x = load(v_ref, (a, b), j)
                before = before_ref[a % 2, b, rows(j), :]
                after = after_ref[a % 2, b, rows(j), :]
                if a >= 2:
                    before, after = pltpu.roll(before, 6, 0), pltpu.roll(after, 2, 0)
                ghost = jnp.where(place < 2, before, after)
                x_m2 = jnp.where(place < 2, ghost, pltpu.roll(x, 2, 0))
                x_m1 = jnp.where(place == 0, pltpu.roll(ghost, 7, 0), pltpu.roll(x, 1, 0))
                x_p1 = jnp.where(place == 3, pltpu.roll(ghost, 1, 0), pltpu.roll(x, 7, 0))
                x_p2 = jnp.where(place >= 2, ghost, pltpu.roll(x, 6, 0))
                (p3, g3), = column([x_m2, x_m1, x, x_p1, x_p2], step_c)
                p1 = load(p1_ref, (a, b), j)
                store(g3_ref, (a, b), j, g3)
                store(m_ref, (a, b), j, p1 * pos_two - p3)
                store(hp_ref, (a, b), j, p1 * drift + p3 * rate + load(h_ref, (a, b), j))


def saturate(x):
    return jnp.sqrt(x) * lax.rsqrt(x + soft)


def last_kernel(
    step_b, lines, upper, final, scal_ref, v_ref, ghost_ref, p1_ref, m_ref, hp_ref,
    drift_ref, *refs,
):
    *most_refs, h_ref, g2_ref, most_ref = refs
    at_edge = scal_ref[27 if upper else 26] > 0.0

    def chunk(j, most):
        drift_one = drift_ref[0, :, wide(j)]
        drift_two = drift_ref[1, :, wide(j)]
        size_one = jnp.abs(drift_one)
        size_two = jnp.abs(drift_two)
        for k, a in enumerate(lines):
            pos_one = scal_ref[a]
            v = [v_ref[a, b, :, wide(j)] for b in range(4)]
            ghost = [ghost_ref[a if ghost_ref.shape[0] == 4 else k, b, :, wide(j)] for b in range(2)]
            if upper:
                v += [
                    jnp.where(at_edge, 2.0 * v[3] - v[2], ghost[0]),
                    jnp.where(at_edge, 3.0 * v[3] - 2.0 * v[2], ghost[1]),
                ]
            else:
                v = [
                    jnp.where(at_edge, 3.0 * v[0] - 2.0 * v[1], ghost[0]),
                    jnp.where(at_edge, 2.0 * v[0] - v[1], ghost[1]),
                ] + v
            for i, (p2, g2) in enumerate(column(v, step_b)):
                b = i + 2 if upper else i
                gust = scal_ref[8 + 4 * a + b]
                g2_ref[k, i, :, wide(j)] = g2
                switch = m_ref[a, b, :, wide(j)] - p2 * pos_one
                square = switch * switch
                y = square + soft
                r = lax.rsqrt(y)
                unit = jnp.abs(switch) * r
                p1 = p1_ref[a, b, :, wide(j)]
                push = (p1 * p1 + p2 * p2) + soft
                wind = gust * lax.rsqrt(push)
                one = size_one + unit * jnp.abs(scal_ref[4 + b]) + jnp.abs(p1) * wind
                two = size_two + unit * jnp.abs(pos_one) + jnp.abs(p2) * wind
                most = (
                    jnp.maximum(most[0], one),
                    jnp.maximum(most[1], two),
                    jnp.maximum(most[2], square),
                )
                hamil = hp_ref[a, b, :, wide(j)] + p2 * drift_two + y * r - wind * push
                h_ref[k, i, :, wide(j)] = hamil
        return most

    if most_refs:
        most = tuple(most_refs[0][i] for i in range(3))
    else:
        most = (jnp.zeros((4, 256), jnp.float32),) * 3
    most = list(lax.fori_loop(0, PAIRS, chunk, most, unroll=5))
    if not final:
        for i in range(3):
            most_ref[i] = most[i]
        return
    lane = lax.broadcasted_iota(jnp.int32, (4, 256), 1)
    spin = jnp.abs(((lane % N6).astype(jnp.float32) - 0.5 * (N6 - 1)) * omega_step)
    most[2] = spin + turn_max * saturate(most[2])
    most += [most_refs[1][i] for i in range(3)]
    row = jnp.zeros((1, LANES), jnp.float32)
    for i, x in enumerate(most):
        x = jnp.max(jnp.max(x, axis=0, keepdims=True), axis=1, keepdims=True)
        row = jnp.where(lane[:1, :LANES] == i, x, row)
    most_ref[...] = jnp.broadcast_to(row, most_ref.shape)


def update_kernel(
    spacings, v_ref, g1_ref, g3_ref, g4_ref, g5_ref, g6_ref, h0_ref, h1_ref, h2_ref,
    g20_ref, g21_ref, g22_ref, most_ref, o_ref, step_ref,
):
    most = jnp.max(most_ref[...], axis=0, keepdims=True)
    lane = lax.broadcasted_iota(jnp.int32, (1, LANES), 1)
    weight = jnp.where(lane == 3, accel_max, jnp.where(lane == 4, other_accel, spin_max))
    speeds = jnp.where(lane < 3, most, weight * saturate(most))
    spacing = jnp.full((1, LANES), spacings[5], jnp.float32)
    for i in range(5):
        spacing = jnp.where(lane == i, spacings[i], spacing)
    per_step = jnp.where(lane < 6, speeds / spacing, 0.0)
    step = courant / jnp.sum(per_step, axis=1, keepdims=True)
    factors = [
        (0.25 * step) * jnp.sum(jnp.where(lane == i, per_step, 0.0), axis=1, keepdims=True)
        for i in range(6)
    ]
    step_ref[...] = step

    for half, h_high, g2_high in ((0, h1_ref, g21_ref), (1, h2_ref, g22_ref)):

        @pl.loop(0, 2)
        def _(k):
            a = 2 * half + k
            for b in range(4):
                for j in range(5):
                    at = (a, b, slice(None), pl.ds(1280 * j, 1280))
                    near = (k, b - 2, slice(None), pl.ds(1280 * j, 1280))
                    h = h0_ref[at] if b < 2 else h_high[near]
                    g2 = g20_ref[at] if b < 2 else g2_high[near]
                    total = v_ref[at] - step * h
                    total = total + factors[0] * g1_ref[at]
                    total = total + factors[1] * g2
                    for f, g_ref in zip(factors[2:], (g3_ref, g4_ref, g5_ref, g6_ref)):
                        total = total + f * g_ref[at]
                    o_ref[at] = total


def edge_codes():
    flat = np.arange(WIDTH).reshape(WIDTH // LANES, 1, LANES)
    flat = np.broadcast_to(flat, (WIDTH // LANES, 4, LANES)).reshape(-1, LANES)
    codes = []
    for stride, count in ((N5 * N6, N4), (N6, N5)):
        place = flat // stride % count
        codes.append(np.where(place == 0, -1, np.where(place == count - 1, 1, 0)))
    return np.stack(codes).astype(np.int32)


def forward(block, axis):
    count = lax.axis_size(axis)
    return lax.ppermute(block, axis, [(i, (i + 1) % count) for i in range(count)])


def backward(block, axis):
    count = lax.axis_size(axis)
    return lax.ppermute(block, axis, [((i + 1) % count, i) for i in range(count)])


def body(value, gust):
    rows_a, rows_b, rows_c, width = value.shape
    axes = ("ga", "gx", "gy")
    count_a = rows_a * lax.axis_size("ga")
    count_b = rows_b * lax.axis_size("gx")
    count_c = rows_c * lax.axis_size("gy")
    step_a = 2.0 * half_span / count_a
    step_b = 2.0 * half_span / count_b
    step_c = 2.0 * math.pi / count_c
    step_four = 1.0 / N4
    step_five = 1.0 / N5
    index_a = lax.axis_index("ga")
    index_b = lax.axis_index("gx")
    index_c = lax.axis_index("gy")

    vmem = pl.BlockSpec(memory_space=pltpu.VMEM)
    hbm = pl.BlockSpec(memory_space=pltpu.HBM)
    smem = pl.BlockSpec(memory_space=pltpu.SMEM)
    full = pltpu.VMEM(value.shape, jnp.float32)
    turn = pltpu.VMEM((2, 4, 4 * width // LANES, LANES), jnp.float32)

    def call(kernel, name, ins, outs, out_specs=None, scratch=()):
        return pl.pallas_call(
            kernel,
            name=name,
            out_shape=tuple(outs),
            in_specs=ins,
            out_specs=tuple(out_specs or [vmem] * len(outs)),
            scratch_shapes=scratch,
            compiler_params=pltpu.CompilerParams(vmem_limit_bytes=8 << 20),
            cost_estimate=pl.CostEstimate(flops=1, bytes_accessed=1, transcendentals=1),
        )

    slab_a = pltpu.VMEM((2, 4, 4, width), jnp.float32)
    slab_b = pltpu.VMEM((4, 2, 4, width), jnp.float32)
    send_high_b = value[:, 2:4]
    low_b = forward(send_high_b, "gx")
    value, send_low_a, send_high_a, send_low_c, send_high_c = call(
        pack_kernel,
        "pack",
        [hbm, hbm],
        [full, slab_a, slab_a, turn, turn],
        scratch=[pltpu.SemaphoreType.DMA],
    )(pltpu.with_memory_space_constraint(value, pltpu.HBM), send_high_b)
    low_c = forward(send_high_c, "gy")
    high_c = backward(send_low_c, "gy")
    low_a = forward(send_high_a, "ga")
    high_a = backward(send_low_a, "ga")

    positions = lax.iota(jnp.int32, width)
    pos_one = -half_span + (
        (index_a * rows_a + lax.iota(jnp.int32, rows_a)).astype(jnp.float32) + 0.5
    ) * step_a
    pos_two = -half_span + (
        (index_b * rows_b + lax.iota(jnp.int32, rows_b)).astype(jnp.float32) + 0.5
    ) * step_b
    heading = (
        -math.pi + (index_c * rows_c + lax.iota(jnp.int32, rows_c)).astype(jnp.float32) * step_c
    ).reshape(rows_c, 1)
    speed_own = 0.5 + ((positions // (N5 * N6)).astype(jnp.float32) + 0.5) * step_four
    speed_other = 0.5 + ((positions // N6 % N5).astype(jnp.float32) + 0.5) * step_five
    drift = jnp.stack(
        [speed_other * jnp.cos(heading) - speed_own, speed_other * jnp.sin(heading)]
    )
    flags = jnp.stack(
        [
            index_a == 0,
            index_a == lax.axis_size("ga") - 1,
            index_b == 0,
            index_b == lax.axis_size("gx") - 1,
        ]
    ).astype(jnp.float32)
    scal = jnp.concatenate([pos_one, pos_two, gust.reshape(-1), flags])

    g4, g5, g6, h_inner, most_inner = call(
        inner_kernel,
        "inner_axes",
        [vmem] * 2,
        [full] * 4 + [pltpu.VMEM((3, 8, LANES), jnp.float32)],
    )(value, jnp.asarray(edge_codes()))
    p1, g1 = call(
        lambda *refs: first_kernel(step_a, *refs),
        "axis_1",
        [smem] + [vmem] * 3,
        [full, full],
    )(scal, value, low_a, high_a)

    slab_b = jax.ShapeDtypeStruct((2, 2, 4, width), jnp.float32)
    send_low_b = call(
        send_kernel,
        "send",
        [vmem] + [hbm] * 3,
        [slab_b, slab_b],
    )(value, low_b, g1, most_inner)
    high_b = [backward(x, "gx") for x in send_low_b]

    m, h_part, g3 = call(
        lambda *refs: third_kernel(step_c, *refs),
        "axis_3",
        [smem] + [vmem] * 6,
        [full] * 3,
    )(scal, value, low_c, high_c, h_inner, p1, drift)

    devices = lax.axis_size(axes)
    inputs = (p1, m, h_part, drift)

    def last(name, lines, upper, ghost, *most):
        part = pltpu.VMEM((len(lines), 2, *value.shape[2:]), jnp.float32)
        final = len(most) > 1
        peaks = (devices, LANES) if final else (3, 4, 256)
        return call(
            lambda *refs: last_kernel(step_b, lines, upper, final, *refs),
            name,
            [smem] + [vmem] * (6 + len(most)),
            [part, part, pltpu.VMEM(peaks, jnp.float32)],
        )(scal, value, ghost, *inputs, *most)

    h0, g20, most = last("rates_0", (0, 1, 2, 3), False, low_b)
    h1, g21, most = last("rates_1", (0, 1), True, high_b[0], most)
    h2, g22, local = last("rates_2", (2, 3), True, high_b[1], most, most_inner)

    spread = lax.all_to_all(local, axes, 0, 0, tiled=True)
    spacings = (step_a, step_b, step_c, step_four, step_five, omega_step)
    value_next, time_step = call(
        lambda *refs: update_kernel(spacings, *refs),
        "update",
        [vmem] * 13,
        [jax.ShapeDtypeStruct(value.shape, jnp.float32), jax.ShapeDtypeStruct((1, 1), jnp.float32)],
    )(value, g1, g3, g4, g5, g6, h0, h1, h2, g20, g21, g22, spread)
    return (value_next, time_step.reshape(1))


def solution(mesh):
    in_specs = (P("ga", "gx", "gy", None), P("ga", "gx"))
    out_specs = (P("ga", "gx", "gy", None), P())
    return jax.shard_map(body, mesh=mesh, in_specs=in_specs, out_specs=out_specs, check_vma=False)
```

```python
import math

import jax
import jax.numpy as jnp
import numpy as np
from jax import lax
from jax.experimental import pallas as pl
from jax.experimental.pallas import tpu as pltpu
from jax.sharding import PartitionSpec as P

N4 = 40
N5 = 40
N6 = 4
WIDTH = N4 * N5 * N6
LANES = 128
PAIRS = WIDTH // (2 * LANES)

turn_max = 1.0
accel_max = 0.5
other_accel = 0.4
spin_max = 0.3
smooth_width = 0.25
courant = 0.5
weno_eps = 1e-06
omega_step = 0.05
half_span = 5.0
soft = smooth_width**2


def lanes(j, half):
    start = 256 * j + 128 * half
    return pl.ds(start if isinstance(j, int) else pl.multiple_of(start, 128), 128)


def load(ref, lead, j):
    return jnp.concatenate(
        [ref[(*lead, slice(None), lanes(j, half))] for half in range(2)], axis=0
    )


def store(ref, lead, j, x):
    ref[(*lead, slice(None), lanes(j, 0))] = x[:4]
    ref[(*lead, slice(None), lanes(j, 1))] = x[4:]


def wide(j):
    return pl.ds(pl.multiple_of(256 * j, 256), 256)


def rows(j):
    return pl.ds(8 * j if isinstance(j, int) else pl.multiple_of(8 * j, 8), 8)


def edge_kernel(v_ref, high_b_ref, sem):
    copy = pltpu.make_async_copy(v_ref.at[:, 2:4], high_b_ref, sem)
    copy.start()
    copy.wait()


def pack_kernel(src_ref, _, v_ref, low_a_ref, high_a_ref, low_c_ref, high_c_ref, sem):
    copy = pltpu.make_async_copy(src_ref, v_ref, sem)
    copy.start()
    copy.wait()
    low_a_ref[...] = v_ref[0:2]
    high_a_ref[...] = v_ref[2:4]
    first = lax.broadcasted_iota(jnp.int32, (8, LANES), 0) % 4 < 2

    @pl.loop(0, 4)
    def _(b):
        for a in range(2):
            for j in range(PAIRS):
                near = load(v_ref, (a, b), j)
                far = load(v_ref, (a + 2, b), j)
                high_c_ref[a, b, rows(j), :] = jnp.where(first, pltpu.roll(near, 6, 0), far)
                low_c_ref[a, b, rows(j), :] = jnp.where(first, far, pltpu.roll(near, 2, 0))


def squared_curve(curve, eps):
    e = curve * curve + eps
    return e * e


def weno(d_back, d_here, s_back, s_here, s_ahead, q_back, q_here, q_ahead, scale):
    u_minus = (s_here - s_back) * (q_here / (q_here + (q_back + q_back)))
    u_plus = (s_ahead - s_here) * (q_here / (q_here + (q_ahead + q_ahead)))
    mean = scale * ((d_back + d_here) - 0.5 * (u_minus + u_plus))
    return mean, u_minus - u_plus


def column(values, spacing):
    eps = weno_eps * spacing**4
    d = [b - a for a, b in zip(values[:-1], values[1:])]
    s = [b - a for a, b in zip(d[:-1], d[1:])]
    q = [squared_curve(x, eps) for x in s]
    return [
        weno(d[i + 1], d[i + 2], s[i], s[i + 1], s[i + 2], q[i], q[i + 1], q[i + 2], 0.5 / spacing)
        for i in range(len(values) - 4)
    ]


def inner_kernel(v_ref, code_ref, g4_ref, g5_ref, g6_ref, h_ref, most_ref):
    lane = lax.broadcasted_iota(jnp.int32, (8, LANES), 1)
    upper = lax.broadcasted_iota(jnp.int32, (8, LANES), 0) < 4
    most_ref[...] = jnp.zeros_like(most_ref)

    def up4(r):
        y = [pltpu.roll(a, 4, 0) for a in r]
        return [jnp.where(upper, y[k], y[(k + 1) % PAIRS]) for k in range(PAIRS)]

    def down4(r):
        y = [pltpu.roll(a, 4, 0) for a in r]
        return [jnp.where(upper, y[k - 1], y[k]) for k in range(PAIRS)]

    def ahead(a, stride):
        n = stride % LANES
        r = [pltpu.roll(y, LANES - n, 1) for y in a]
        if stride == 1:
            return r
        u = up4(r)
        near, far = (r, u) if stride < LANES else (u, r[1:] + r[:1])
        return [jnp.where(lane < LANES - n, near[k], far[k]) for k in range(PAIRS)]

    def back(a, stride):
        n = stride % LANES
        r = [pltpu.roll(y, n, 1) for y in a]
        if stride == 1:
            return r
        u = down4(r)
        near, far = (r, u) if stride < LANES else (u, r[-1:] + r[:-1])
        return [jnp.where(lane >= n, near[k], far[k]) for k in range(PAIRS)]

    @pl.loop(0, 16)
    def _(line):
        lead = (lax.div(line, 4), lax.rem(line, 4))
        x = [load(v_ref, lead, j) for j in range(PAIRS)]
        total = [None] * PAIRS
        for stride, spacing, weight, g_ref, which in (
            (N5 * N6, 1.0 / N4, accel_max, g4_ref, 0),
            (N6, 1.0 / N5, -other_accel, g5_ref, 1),
            (1, omega_step, -spin_max, g6_ref, 2),
        ):
            eps = weno_eps * spacing**4
            if which < 2:
                codes = [code_ref[which, rows(k), :] for k in range(PAIRS)]
            else:
                place = lane % N6
                codes = [jnp.where(place == 0, -1, jnp.where(place == N6 - 1, 1, 0))] * PAIRS
            d = [b - a for a, b in zip(x, ahead(x, stride))]
            before = [a - b for a, b in zip(x, back(x, stride))]
            d_here = [jnp.where(c > 0, b, a) for c, a, b in zip(codes, d, before)]
            d_back = [jnp.where(c < 0, a, b) for c, a, b in zip(codes, d, before)]
            s = [a - b for a, b in zip(d_here, d_back)]
            s_ahead = ahead(s, stride)
            s_back = back(s, stride)
            peak = None
            for k in range(PAIRS):
                mean, diff = weno(
                    d_back[k],
                    d_here[k],
                    s_back[k],
                    s[k],
                    s_ahead[k],
                    squared_curve(s_back[k], eps),
                    squared_curve(s[k], eps),
                    squared_curve(s_ahead[k], eps),
                    0.5 / spacing,
                )
                store(g_ref, lead, k, diff)
                square = mean * mean
                peak = square if peak is None else jnp.maximum(peak, square)
                y = square + soft
                root = weight * (y * lax.rsqrt(y))
                total[k] = root if total[k] is None else total[k] + root
            most_ref[which] = jnp.maximum(most_ref[which], peak)
        for k in range(PAIRS):
            store(h_ref, lead, k, total[k])


def send_kernel(v_ref, *refs):
    low_b0_ref, low_b1_ref = refs[-2:]
    low_b0_ref[...] = v_ref[0:2, 0:2]
    low_b1_ref[...] = v_ref[2:4, 0:2]


def first_kernel(step_a, scal_ref, v_ref, low_ref, high_ref, p1_ref, g1_ref):
    at_low = scal_ref[24] > 0.0
    at_high = scal_ref[25] > 0.0

    @pl.loop(0, PAIRS)
    def _(j):
        for b in range(4):
            v = [v_ref[a, b, :, wide(j)] for a in range(4)]
            low = [low_ref[a, b, :, wide(j)] for a in range(2)]
            high = [high_ref[a, b, :, wide(j)] for a in range(2)]
            low = [
                jnp.where(at_low, 3.0 * v[0] - 2.0 * v[1], low[0]),
                jnp.where(at_low, 2.0 * v[0] - v[1], low[1]),
            ]
            high = [
                jnp.where(at_high, 2.0 * v[3] - v[2], high[0]),
                jnp.where(at_high, 3.0 * v[3] - 2.0 * v[2], high[1]),
            ]
            for a, (p1, g1) in enumerate(column(low + v + high, step_a)):
                p1_ref[a, b, :, wide(j)] = p1
                g1_ref[a, b, :, wide(j)] = g1


def third_kernel(
    step_c, scal_ref, v_ref, before_ref, after_ref, h_ref, p1_ref, drift_ref,
    m_ref, hp_ref, g3_ref,
):
    place = lax.broadcasted_iota(jnp.int32, (8, LANES), 0) % 4
    rate = (
        (lax.broadcasted_iota(jnp.int32, (8, LANES), 1) % N6).astype(jnp.float32)
        - 0.5 * (N6 - 1)
    ) * omega_step

    @pl.loop(0, PAIRS)
    def _(j):
        drift = load(drift_ref, (0,), j)
        for b in range(4):
            pos_two = scal_ref[4 + b]
            for a in range(4):
                x = load(v_ref, (a, b), j)
                before = before_ref[a % 2, b, rows(j), :]
                after = after_ref[a % 2, b, rows(j), :]
                if a >= 2:
                    before, after = pltpu.roll(before, 6, 0), pltpu.roll(after, 2, 0)
                ghost = jnp.where(place < 2, before, after)
                x_m2 = jnp.where(place < 2, ghost, pltpu.roll(x, 2, 0))
                x_m1 = jnp.where(place == 0, pltpu.roll(ghost, 7, 0), pltpu.roll(x, 1, 0))
                x_p1 = jnp.where(place == 3, pltpu.roll(ghost, 1, 0), pltpu.roll(x, 7, 0))
                x_p2 = jnp.where(place >= 2, ghost, pltpu.roll(x, 6, 0))
                (p3, g3), = column([x_m2, x_m1, x, x_p1, x_p2], step_c)
                p1 = load(p1_ref, (a, b), j)
                store(g3_ref, (a, b), j, g3)
                store(m_ref, (a, b), j, p1 * pos_two - p3)
                store(hp_ref, (a, b), j, p1 * drift + p3 * rate + load(h_ref, (a, b), j))


def saturate(x):
    return jnp.sqrt(x) * lax.rsqrt(x + soft)


def last_kernel(
    step_b, lines, upper, final, scal_ref, v_ref, ghost_ref, p1_ref, m_ref, hp_ref,
    drift_ref, *refs,
):
    *most_refs, h_ref, g2_ref, most_ref = refs
    if not upper:
        most_refs, h_ref, g2_ref, most_ref = (refs[0], refs[4]), *refs[1:4]
    at_edge = scal_ref[27 if upper else 26] > 0.0

    def chunk(j, most):
        drift_one = drift_ref[0, :, wide(j)]
        drift_two = drift_ref[1, :, wide(j)]
        size_one = jnp.abs(drift_one)
        size_two = jnp.abs(drift_two)
        for k, a in enumerate(lines):
            pos_one = scal_ref[a]
            v = [v_ref[a, b, :, wide(j)] for b in range(4)]
            ghost = [ghost_ref[a if ghost_ref.shape[0] == 4 else k, b, :, wide(j)] for b in range(2)]
            if upper:
                v += [
                    jnp.where(at_edge, 2.0 * v[3] - v[2], ghost[0]),
                    jnp.where(at_edge, 3.0 * v[3] - 2.0 * v[2], ghost[1]),
                ]
            else:
                v = [
                    jnp.where(at_edge, 3.0 * v[0] - 2.0 * v[1], ghost[0]),
                    jnp.where(at_edge, 2.0 * v[0] - v[1], ghost[1]),
                ] + v
            for i, (p2, g2) in enumerate(column(v, step_b)):
                b = i + 2 if upper else i
                gust = scal_ref[8 + 4 * a + b]
                g2_ref[k, i, :, wide(j)] = g2
                switch = m_ref[a, b, :, wide(j)] - p2 * pos_one
                square = switch * switch
                y = square + soft
                r = lax.rsqrt(y)
                unit = jnp.abs(switch) * r
                p1 = p1_ref[a, b, :, wide(j)]
                push = (p1 * p1 + p2 * p2) + soft
                wind = gust * lax.rsqrt(push)
                one = size_one + unit * jnp.abs(scal_ref[4 + b]) + jnp.abs(p1) * wind
                two = size_two + unit * jnp.abs(pos_one) + jnp.abs(p2) * wind
                most = (
                    jnp.maximum(most[0], one),
                    jnp.maximum(most[1], two),
                    jnp.maximum(most[2], square),
                )
                hamil = hp_ref[a, b, :, wide(j)] + p2 * drift_two + y * r - wind * push
                h_ref[k, i, :, wide(j)] = hamil
        return most

    def row_of(arrays, start):
        lane = lax.broadcasted_iota(jnp.int32, (1, LANES), 1)
        row = jnp.zeros((1, LANES), jnp.float32)
        for i, x in enumerate(arrays):
            x = jnp.max(jnp.max(x, axis=0, keepdims=True), axis=1, keepdims=True)
            row = jnp.where(lane == start + i, x, row)
        return row

    if upper:
        most = tuple(most_refs[0][i] for i in range(3))
    else:
        most = (jnp.zeros((4, 256), jnp.float32),) * 3
    most = list(lax.fori_loop(0, PAIRS, chunk, most, unroll=5))
    if not final:
        for i in range(3):
            most_ref[i] = most[i]
        if not upper:
            most_refs[1][...] = row_of([most_refs[0][i] for i in range(3)], 3)
        return
    lane = lax.broadcasted_iota(jnp.int32, (4, 256), 1)
    spin = jnp.abs(((lane % N6).astype(jnp.float32) - 0.5 * (N6 - 1)) * omega_step)
    most[2] = spin + turn_max * saturate(most[2])
    row = row_of(most, 0) + most_refs[1][...]
    most_ref[...] = jnp.broadcast_to(row, most_ref.shape)


def update_kernel(
    spacings, v_ref, g1_ref, g3_ref, g4_ref, g5_ref, g6_ref, h0_ref, h1_ref, h2_ref,
    g20_ref, g21_ref, g22_ref, most_ref, o_ref, step_ref,
):
    most = jnp.max(most_ref[...], axis=0, keepdims=True)
    lane = lax.broadcasted_iota(jnp.int32, (1, LANES), 1)
    weight = jnp.where(lane == 3, accel_max, jnp.where(lane == 4, other_accel, spin_max))
    speeds = jnp.where(lane < 3, most, weight * saturate(most))
    spacing = jnp.full((1, LANES), spacings[5], jnp.float32)
    for i in range(5):
        spacing = jnp.where(lane == i, spacings[i], spacing)
    per_step = jnp.where(lane < 6, speeds / spacing, 0.0)
    step = courant / jnp.sum(per_step, axis=1, keepdims=True)
    factors = [
        (0.25 * step) * jnp.sum(jnp.where(lane == i, per_step, 0.0), axis=1, keepdims=True)
        for i in range(6)
    ]
    step_ref[...] = step

    for half, h_high, g2_high in ((0, h1_ref, g21_ref), (1, h2_ref, g22_ref)):

        @pl.loop(0, 2)
        def _(k):
            a = 2 * half + k
            for b in range(4):
                for j in range(5):
                    at = (a, b, slice(None), pl.ds(1280 * j, 1280))
                    near = (k, b - 2, slice(None), pl.ds(1280 * j, 1280))
                    h = h0_ref[at] if b < 2 else h_high[near]
                    g2 = g20_ref[at] if b < 2 else g2_high[near]
                    total = v_ref[at] - step * h
                    total = total + factors[0] * g1_ref[at]
                    total = total + factors[1] * g2
                    for f, g_ref in zip(factors[2:], (g3_ref, g4_ref, g5_ref, g6_ref)):
                        total = total + f * g_ref[at]
                    o_ref[at] = total


def edge_codes():
    flat = np.arange(WIDTH).reshape(WIDTH // LANES, 1, LANES)
    flat = np.broadcast_to(flat, (WIDTH // LANES, 4, LANES)).reshape(-1, LANES)
    codes = []
    for stride, count in ((N5 * N6, N4), (N6, N5)):
        place = flat // stride % count
        codes.append(np.where(place == 0, -1, np.where(place == count - 1, 1, 0)))
    return np.stack(codes).astype(np.int32)


def forward(block, axis):
    count = lax.axis_size(axis)
    return lax.ppermute(block, axis, [(i, (i + 1) % count) for i in range(count)])


def backward(block, axis):
    count = lax.axis_size(axis)
    return lax.ppermute(block, axis, [((i + 1) % count, i) for i in range(count)])


def body(value, gust):
    rows_a, rows_b, rows_c, width = value.shape
    axes = ("ga", "gx", "gy")
    count_a = rows_a * lax.axis_size("ga")
    count_b = rows_b * lax.axis_size("gx")
    count_c = rows_c * lax.axis_size("gy")
    step_a = 2.0 * half_span / count_a
    step_b = 2.0 * half_span / count_b
    step_c = 2.0 * math.pi / count_c
    step_four = 1.0 / N4
    step_five = 1.0 / N5
    index_a = lax.axis_index("ga")
    index_b = lax.axis_index("gx")
    index_c = lax.axis_index("gy")

    vmem = pl.BlockSpec(memory_space=pltpu.VMEM)
    hbm = pl.BlockSpec(memory_space=pltpu.HBM)
    smem = pl.BlockSpec(memory_space=pltpu.SMEM)
    full = pltpu.VMEM(value.shape, jnp.float32)
    turn = pltpu.VMEM((2, 4, 4 * width // LANES, LANES), jnp.float32)

    def call(kernel, name, ins, outs, out_specs=None, scratch=()):
        return pl.pallas_call(
            kernel,
            name=name,
            out_shape=tuple(outs),
            in_specs=ins,
            out_specs=tuple(out_specs or [vmem] * len(outs)),
            scratch_shapes=scratch,
            compiler_params=pltpu.CompilerParams(vmem_limit_bytes=8 << 20),
            cost_estimate=pl.CostEstimate(flops=1, bytes_accessed=1, transcendentals=1),
        )

    slab_a = pltpu.VMEM((2, 4, 4, width), jnp.float32)
    slab_b = pltpu.VMEM((4, 2, 4, width), jnp.float32)
    (send_high_b,) = call(
        edge_kernel,
        "edge",
        [hbm],
        [pltpu.VMEM((4, 2, 4, width), jnp.float32)],
        scratch=[pltpu.SemaphoreType.DMA],
    )(pltpu.with_memory_space_constraint(value, pltpu.HBM))
    low_b = forward(send_high_b, "gx")
    value, send_low_a, send_high_a, send_low_c, send_high_c = call(
        pack_kernel,
        "pack",
        [hbm, hbm],
        [full, slab_a, slab_a, turn, turn],
        scratch=[pltpu.SemaphoreType.DMA],
    )(pltpu.with_memory_space_constraint(value, pltpu.HBM), send_high_b)
    low_c = forward(send_high_c, "gy")
    high_c = backward(send_low_c, "gy")
    low_a = forward(send_high_a, "ga")
    high_a = backward(send_low_a, "ga")

    positions = lax.iota(jnp.int32, width)
    pos_one = -half_span + (
        (index_a * rows_a + lax.iota(jnp.int32, rows_a)).astype(jnp.float32) + 0.5
    ) * step_a
    pos_two = -half_span + (
        (index_b * rows_b + lax.iota(jnp.int32, rows_b)).astype(jnp.float32) + 0.5
    ) * step_b
    heading = (
        -math.pi + (index_c * rows_c + lax.iota(jnp.int32, rows_c)).astype(jnp.float32) * step_c
    ).reshape(rows_c, 1)
    speed_own = 0.5 + ((positions // (N5 * N6)).astype(jnp.float32) + 0.5) * step_four
    speed_other = 0.5 + ((positions // N6 % N5).astype(jnp.float32) + 0.5) * step_five
    drift = jnp.stack(
        [speed_other * jnp.cos(heading) - speed_own, speed_other * jnp.sin(heading)]
    )
    flags = jnp.stack(
        [
            index_a == 0,
            index_a == lax.axis_size("ga") - 1,
            index_b == 0,
            index_b == lax.axis_size("gx") - 1,
        ]
    ).astype(jnp.float32)
    scal = jnp.concatenate([pos_one, pos_two, gust.reshape(-1), flags])

    g4, g5, g6, h_inner, most_inner = call(
        inner_kernel,
        "inner_axes",
        [vmem] * 2,
        [full] * 4 + [pltpu.VMEM((3, 8, LANES), jnp.float32)],
    )(value, jnp.asarray(edge_codes()))
    p1, g1 = call(
        lambda *refs: first_kernel(step_a, *refs),
        "axis_1",
        [smem] + [vmem] * 3,
        [full, full],
    )(scal, value, low_a, high_a)

    slab_b = jax.ShapeDtypeStruct((2, 2, 4, width), jnp.float32)
    send_low_b = call(
        send_kernel,
        "send",
        [vmem] + [hbm] * 3,
        [slab_b, slab_b],
    )(value, low_b, g1, most_inner)
    high_b = [backward(x, "gx") for x in send_low_b]

    m, h_part, g3 = call(
        lambda *refs: third_kernel(step_c, *refs),
        "axis_3",
        [smem] + [vmem] * 6,
        [full] * 3,
    )(scal, value, low_c, high_c, h_inner, p1, drift)

    devices = lax.axis_size(axes)
    inputs = (p1, m, h_part, drift)

    def last(name, lines, upper, ghost, *most):
        part = pltpu.VMEM((len(lines), 2, *value.shape[2:]), jnp.float32)
        final = len(most) > 1
        peaks = [pltpu.VMEM((devices, LANES) if final else (3, 4, 256), jnp.float32)]
        if not upper:
            peaks.append(pltpu.VMEM((1, LANES), jnp.float32))
        return call(
            lambda *refs: last_kernel(step_b, lines, upper, final, *refs),
            name,
            [smem] + [vmem] * (6 + len(most)),
            [part, part] + peaks,
        )(scal, value, ghost, *inputs, *most)

    h0, g20, most, row = last("rates_0", (0, 1, 2, 3), False, low_b, most_inner)
    h1, g21, most = last("rates_1", (0, 1), True, high_b[0], most)
    h2, g22, local = last("rates_2", (2, 3), True, high_b[1], most, row)

    spread = lax.all_to_all(local, axes, 0, 0, tiled=True)
    spacings = (step_a, step_b, step_c, step_four, step_five, omega_step)
    value_next, time_step = call(
        lambda *refs: update_kernel(spacings, *refs),
        "update",
        [vmem] * 13,
        [jax.ShapeDtypeStruct(value.shape, jnp.float32), jax.ShapeDtypeStruct((1, 1), jnp.float32)],
    )(value, g1, g3, g4, g5, g6, h0, h1, h2, g20, g21, g22, spread)
    return (value_next, time_step.reshape(1))


def solution(mesh):
    in_specs = (P("ga", "gx", "gy", None), P("ga", "gx"))
    out_specs = (P("ga", "gx", "gy", None), P())
    return jax.shard_map(body, mesh=mesh, in_specs=in_specs, out_specs=out_specs, check_vma=False)
```

```python
import math

import jax
import jax.numpy as jnp
import numpy as np
from jax import lax
from jax.experimental import pallas as pl
from jax.experimental.pallas import tpu as pltpu
from jax.sharding import PartitionSpec as P

N4 = 40
N5 = 40
N6 = 4
WIDTH = N4 * N5 * N6
LANES = 128
PAIRS = WIDTH // (2 * LANES)

turn_max = 1.0
accel_max = 0.5
other_accel = 0.4
spin_max = 0.3
smooth_width = 0.25
courant = 0.5
weno_eps = 1e-06
omega_step = 0.05
half_span = 5.0
soft = smooth_width**2


def lanes(j, half):
    start = 256 * j + 128 * half
    return pl.ds(start if isinstance(j, int) else pl.multiple_of(start, 128), 128)


def load(ref, lead, j):
    return jnp.concatenate(
        [ref[(*lead, slice(None), lanes(j, half))] for half in range(2)], axis=0
    )


def store(ref, lead, j, x):
    ref[(*lead, slice(None), lanes(j, 0))] = x[:4]
    ref[(*lead, slice(None), lanes(j, 1))] = x[4:]


def wide(j):
    return pl.ds(pl.multiple_of(256 * j, 256), 256)


def rows(j):
    return pl.ds(8 * j if isinstance(j, int) else pl.multiple_of(8 * j, 8), 8)


def pack_kernel(src_ref, _, v_ref, low_a_ref, high_a_ref, low_c_ref, high_c_ref, sem):
    copy = pltpu.make_async_copy(src_ref, v_ref, sem)
    copy.start()
    copy.wait()
    low_a_ref[...] = v_ref[0:2]
    high_a_ref[...] = v_ref[2:4]
    first = lax.broadcasted_iota(jnp.int32, (8, LANES), 0) % 4 < 2

    @pl.loop(0, 4)
    def _(b):
        for a in range(2):
            for j in range(PAIRS):
                near = load(v_ref, (a, b), j)
                far = load(v_ref, (a + 2, b), j)
                high_c_ref[a, b, rows(j), :] = jnp.where(first, pltpu.roll(near, 6, 0), far)
                low_c_ref[a, b, rows(j), :] = jnp.where(first, far, pltpu.roll(near, 2, 0))


def squared_curve(curve, eps):
    e = curve * curve + eps
    return e * e


def weno(d_back, d_here, s_back, s_here, s_ahead, q_back, q_here, q_ahead, scale):
    u_minus = (s_here - s_back) * (q_here / (q_here + (q_back + q_back)))
    u_plus = (s_ahead - s_here) * (q_here / (q_here + (q_ahead + q_ahead)))
    mean = scale * ((d_back + d_here) - 0.5 * (u_minus + u_plus))
    return mean, u_minus - u_plus


def column(values, spacing):
    eps = weno_eps * spacing**4
    d = [b - a for a, b in zip(values[:-1], values[1:])]
    s = [b - a for a, b in zip(d[:-1], d[1:])]
    q = [squared_curve(x, eps) for x in s]
    return [
        weno(d[i + 1], d[i + 2], s[i], s[i + 1], s[i + 2], q[i], q[i + 1], q[i + 2], 0.5 / spacing)
        for i in range(len(values) - 4)
    ]


def inner_kernel(v_ref, code_ref, g4_ref, g5_ref, g6_ref, h_ref, most_ref):
    lane = lax.broadcasted_iota(jnp.int32, (8, LANES), 1)
    upper = lax.broadcasted_iota(jnp.int32, (8, LANES), 0) < 4
    most_ref[...] = jnp.zeros_like(most_ref)

    def up4(r):
        y = [pltpu.roll(a, 4, 0) for a in r]
        return [jnp.where(upper, y[k], y[(k + 1) % PAIRS]) for k in range(PAIRS)]

    def down4(r):
        y = [pltpu.roll(a, 4, 0) for a in r]
        return [jnp.where(upper, y[k - 1], y[k]) for k in range(PAIRS)]

    def ahead(a, stride):
        n = stride % LANES
        r = [pltpu.roll(y, LANES - n, 1) for y in a]
        if stride == 1:
            return r
        u = up4(r)
        near, far = (r, u) if stride < LANES else (u, r[1:] + r[:1])
        return [jnp.where(lane < LANES - n, near[k], far[k]) for k in range(PAIRS)]

    def back(a, stride):
        n = stride % LANES
        r = [pltpu.roll(y, n, 1) for y in a]
        if stride == 1:
            return r
        u = down4(r)
        near, far = (r, u) if stride < LANES else (u, r[-1:] + r[:-1])
        return [jnp.where(lane >= n, near[k], far[k]) for k in range(PAIRS)]

    @pl.loop(0, 16)
    def _(line):
        lead = (lax.div(line, 4), lax.rem(line, 4))
        x = [load(v_ref, lead, j) for j in range(PAIRS)]
        total = [None] * PAIRS
        for stride, spacing, weight, g_ref, which in (
            (N5 * N6, 1.0 / N4, accel_max, g4_ref, 0),
            (N6, 1.0 / N5, -other_accel, g5_ref, 1),
            (1, omega_step, -spin_max, g6_ref, 2),
        ):
            eps = weno_eps * spacing**4
            if which < 2:
                codes = [code_ref[which, rows(k), :] for k in range(PAIRS)]
            else:
                place = lane % N6
                codes = [jnp.where(place == 0, -1, jnp.where(place == N6 - 1, 1, 0))] * PAIRS
            d = [b - a for a, b in zip(x, ahead(x, stride))]
            before = [a - b for a, b in zip(x, back(x, stride))]
            d_here = [jnp.where(c > 0, b, a) for c, a, b in zip(codes, d, before)]
            d_back = [jnp.where(c < 0, a, b) for c, a, b in zip(codes, d, before)]
            s = [a - b for a, b in zip(d_here, d_back)]
            s_ahead = ahead(s, stride)
            s_back = back(s, stride)
            peak = None
            for k in range(PAIRS):
                mean, diff = weno(
                    d_back[k],
                    d_here[k],
                    s_back[k],
                    s[k],
                    s_ahead[k],
                    squared_curve(s_back[k], eps),
                    squared_curve(s[k], eps),
                    squared_curve(s_ahead[k], eps),
                    0.5 / spacing,
                )
                store(g_ref, lead, k, diff)
                square = mean * mean
                peak = square if peak is None else jnp.maximum(peak, square)
                y = square + soft
                root = weight * (y * lax.rsqrt(y))
                total[k] = root if total[k] is None else total[k] + root
            most_ref[which] = jnp.maximum(most_ref[which], peak)
        for k in range(PAIRS):
            store(h_ref, lead, k, total[k])


def send_kernel(v_ref, *refs):
    low_b0_ref, low_b1_ref = refs[-2:]
    low_b0_ref[...] = v_ref[0:2, 0:2]
    low_b1_ref[...] = v_ref[2:4, 0:2]


def first_kernel(step_a, scal_ref, v_ref, low_ref, high_ref, p1_ref, g1_ref):
    at_low = scal_ref[24] > 0.0
    at_high = scal_ref[25] > 0.0

    @pl.loop(0, PAIRS)
    def _(j):
        for b in range(4):
            v = [v_ref[a, b, :, wide(j)] for a in range(4)]
            low = [low_ref[a, b, :, wide(j)] for a in range(2)]
            high = [high_ref[a, b, :, wide(j)] for a in range(2)]
            low = [
                jnp.where(at_low, 3.0 * v[0] - 2.0 * v[1], low[0]),
                jnp.where(at_low, 2.0 * v[0] - v[1], low[1]),
            ]
            high = [
                jnp.where(at_high, 2.0 * v[3] - v[2], high[0]),
                jnp.where(at_high, 3.0 * v[3] - 2.0 * v[2], high[1]),
            ]
            for a, (p1, g1) in enumerate(column(low + v + high, step_a)):
                p1_ref[a, b, :, wide(j)] = p1
                g1_ref[a, b, :, wide(j)] = g1


def third_kernel(
    step_c, scal_ref, v_ref, before_ref, after_ref, h_ref, p1_ref, drift_ref,
    m_ref, hp_ref, g3_ref,
):
    place = lax.broadcasted_iota(jnp.int32, (8, LANES), 0) % 4
    rate = (
        (lax.broadcasted_iota(jnp.int32, (8, LANES), 1) % N6).astype(jnp.float32)
        - 0.5 * (N6 - 1)
    ) * omega_step

    @pl.loop(0, PAIRS)
    def _(j):
        drift = load(drift_ref, (0,), j)
        for b in range(4):
            pos_two = scal_ref[4 + b]
            for a in range(4):
                x = load(v_ref, (a, b), j)
                before = before_ref[a % 2, b, rows(j), :]
                after = after_ref[a % 2, b, rows(j), :]
                if a >= 2:
                    before, after = pltpu.roll(before, 6, 0), pltpu.roll(after, 2, 0)
                ghost = jnp.where(place < 2, before, after)
                x_m2 = jnp.where(place < 2, ghost, pltpu.roll(x, 2, 0))
                x_m1 = jnp.where(place == 0, pltpu.roll(ghost, 7, 0), pltpu.roll(x, 1, 0))
                x_p1 = jnp.where(place == 3, pltpu.roll(ghost, 1, 0), pltpu.roll(x, 7, 0))
                x_p2 = jnp.where(place >= 2, ghost, pltpu.roll(x, 6, 0))
                (p3, g3), = column([x_m2, x_m1, x, x_p1, x_p2], step_c)
                p1 = load(p1_ref, (a, b), j)
                store(g3_ref, (a, b), j, g3)
                store(m_ref, (a, b), j, p1 * pos_two - p3)
                store(hp_ref, (a, b), j, p1 * drift + p3 * rate + load(h_ref, (a, b), j))


def saturate(x):
    return jnp.sqrt(x) * lax.rsqrt(x + soft)


def last_kernel(
    step_b, lines, upper, final, scal_ref, v_ref, ghost_ref, p1_ref, m_ref, hp_ref,
    drift_ref, *refs,
):
    *most_refs, h_ref, g2_ref, most_ref = refs
    at_edge = scal_ref[27 if upper else 26] > 0.0

    def chunk(j, most):
        drift_one = drift_ref[0, :, wide(j)]
        drift_two = drift_ref[1, :, wide(j)]
        size_one = jnp.abs(drift_one)
        size_two = jnp.abs(drift_two)
        for k, a in enumerate(lines):
            pos_one = scal_ref[a]
            v = [v_ref[a, b, :, wide(j)] for b in range(4)]
            ghost = [ghost_ref[a if ghost_ref.shape[0] == 4 else k, b, :, wide(j)] for b in range(2)]
            if upper:
                v += [
                    jnp.where(at_edge, 2.0 * v[3] - v[2], ghost[0]),
                    jnp.where(at_edge, 3.0 * v[3] - 2.0 * v[2], ghost[1]),
                ]
            else:
                v = [
                    jnp.where(at_edge, 3.0 * v[0] - 2.0 * v[1], ghost[0]),
                    jnp.where(at_edge, 2.0 * v[0] - v[1], ghost[1]),
                ] + v
            for i, (p2, g2) in enumerate(column(v, step_b)):
                b = i + 2 if upper else i
                gust = scal_ref[8 + 4 * a + b]
                g2_ref[k, i, :, wide(j)] = g2
                switch = m_ref[a, b, :, wide(j)] - p2 * pos_one
                square = switch * switch
                y = square + soft
                r = lax.rsqrt(y)
                unit = jnp.abs(switch) * r
                p1 = p1_ref[a, b, :, wide(j)]
                push = (p1 * p1 + p2 * p2) + soft
                wind = gust * lax.rsqrt(push)
                one = size_one + unit * jnp.abs(scal_ref[4 + b]) + jnp.abs(p1) * wind
                two = size_two + unit * jnp.abs(pos_one) + jnp.abs(p2) * wind
                most = (
                    jnp.maximum(most[0], one),
                    jnp.maximum(most[1], two),
                    jnp.maximum(most[2], square),
                )
                hamil = hp_ref[a, b, :, wide(j)] + p2 * drift_two + y * r - wind * push
                h_ref[k, i, :, wide(j)] = hamil
        return most

    if most_refs:
        most = tuple(most_refs[0][i] for i in range(3))
    else:
        most = (jnp.zeros((4, 256), jnp.float32),) * 3
    most = list(lax.fori_loop(0, PAIRS, chunk, most, unroll=5))
    if not final:
        for i in range(3):
            most_ref[i] = most[i]
        return
    lane = lax.broadcasted_iota(jnp.int32, (4, 256), 1)
    spin = jnp.abs(((lane % N6).astype(jnp.float32) - 0.5 * (N6 - 1)) * omega_step)
    most[2] = spin + turn_max * saturate(most[2])
    most += [most_refs[1][i] for i in range(3)]
    row = jnp.zeros((1, LANES), jnp.float32)
    for i, x in enumerate(most):
        x = jnp.max(jnp.max(x, axis=0, keepdims=True), axis=1, keepdims=True)
        row = jnp.where(lane[:1, :LANES] == i, x, row)
    most_ref[...] = jnp.broadcast_to(row, most_ref.shape)


def update_kernel(
    spacings, v_ref, g1_ref, g3_ref, g4_ref, g5_ref, g6_ref, h0_ref, h1_ref, h2_ref,
    g20_ref, g21_ref, g22_ref, most_ref, o_ref, step_ref,
):
    most = jnp.max(most_ref[...], axis=0, keepdims=True)
    lane = lax.broadcasted_iota(jnp.int32, (1, LANES), 1)
    weight = jnp.where(lane == 3, accel_max, jnp.where(lane == 4, other_accel, spin_max))
    speeds = jnp.where(lane < 3, most, weight * saturate(most))
    spacing = jnp.full((1, LANES), spacings[5], jnp.float32)
    for i in range(5):
        spacing = jnp.where(lane == i, spacings[i], spacing)
    per_step = jnp.where(lane < 6, speeds / spacing, 0.0)
    step = courant / jnp.sum(per_step, axis=1, keepdims=True)
    factors = [
        (0.25 * step) * jnp.sum(jnp.where(lane == i, per_step, 0.0), axis=1, keepdims=True)
        for i in range(6)
    ]
    step_ref[...] = step

    for half, h_high, g2_high in ((0, h1_ref, g21_ref), (1, h2_ref, g22_ref)):

        @pl.loop(0, 2)
        def _(k):
            a = 2 * half + k
            for b in range(4):
                for j in range(5):
                    at = (a, b, slice(None), pl.ds(1280 * j, 1280))
                    near = (k, b - 2, slice(None), pl.ds(1280 * j, 1280))
                    h = h0_ref[at] if b < 2 else h_high[near]
                    g2 = g20_ref[at] if b < 2 else g2_high[near]
                    total = v_ref[at] - step * h
                    total = total + factors[0] * g1_ref[at]
                    total = total + factors[1] * g2
                    for f, g_ref in zip(factors[2:], (g3_ref, g4_ref, g5_ref, g6_ref)):
                        total = total + f * g_ref[at]
                    o_ref[at] = total


def edge_codes():
    flat = np.arange(WIDTH).reshape(WIDTH // LANES, 1, LANES)
    flat = np.broadcast_to(flat, (WIDTH // LANES, 4, LANES)).reshape(-1, LANES)
    codes = []
    for stride, count in ((N5 * N6, N4), (N6, N5)):
        place = flat // stride % count
        codes.append(np.where(place == 0, -1, np.where(place == count - 1, 1, 0)))
    return np.stack(codes).astype(np.int32)


def forward(block, axis):
    count = lax.axis_size(axis)
    pairs = count if axis == "gy" else count - 1
    return lax.ppermute(block, axis, [(i, (i + 1) % count) for i in range(pairs)])


def backward(block, axis):
    count = lax.axis_size(axis)
    pairs = count if axis == "gy" else count - 1
    return lax.ppermute(block, axis, [((i + 1) % count, i) for i in range(pairs)])


def body(value, gust):
    rows_a, rows_b, rows_c, width = value.shape
    axes = ("ga", "gx", "gy")
    count_a = rows_a * lax.axis_size("ga")
    count_b = rows_b * lax.axis_size("gx")
    count_c = rows_c * lax.axis_size("gy")
    step_a = 2.0 * half_span / count_a
    step_b = 2.0 * half_span / count_b
    step_c = 2.0 * math.pi / count_c
    step_four = 1.0 / N4
    step_five = 1.0 / N5
    index_a = lax.axis_index("ga")
    index_b = lax.axis_index("gx")
    index_c = lax.axis_index("gy")

    vmem = pl.BlockSpec(memory_space=pltpu.VMEM)
    hbm = pl.BlockSpec(memory_space=pltpu.HBM)
    smem = pl.BlockSpec(memory_space=pltpu.SMEM)
    full = pltpu.VMEM(value.shape, jnp.float32)
    turn = pltpu.VMEM((2, 4, 4 * width // LANES, LANES), jnp.float32)

    def call(kernel, name, ins, outs, out_specs=None, scratch=()):
        return pl.pallas_call(
            kernel,
            name=name,
            out_shape=tuple(outs),
            in_specs=ins,
            out_specs=tuple(out_specs or [vmem] * len(outs)),
            scratch_shapes=scratch,
            compiler_params=pltpu.CompilerParams(vmem_limit_bytes=8 << 20),
            cost_estimate=pl.CostEstimate(flops=1, bytes_accessed=1, transcendentals=1),
        )

    slab_a = pltpu.VMEM((2, 4, 4, width), jnp.float32)
    slab_b = pltpu.VMEM((4, 2, 4, width), jnp.float32)
    send_high_b = value[:, 2:4]
    low_b = forward(send_high_b, "gx")
    value, send_low_a, send_high_a, send_low_c, send_high_c = call(
        pack_kernel,
        "pack",
        [hbm, hbm],
        [full, slab_a, slab_a, turn, turn],
        scratch=[pltpu.SemaphoreType.DMA],
    )(pltpu.with_memory_space_constraint(value, pltpu.HBM), send_high_b)
    low_c = forward(send_high_c, "gy")
    high_c = backward(send_low_c, "gy")
    low_a = forward(send_high_a, "ga")
    high_a = backward(send_low_a, "ga")

    positions = lax.iota(jnp.int32, width)
    pos_one = -half_span + (
        (index_a * rows_a + lax.iota(jnp.int32, rows_a)).astype(jnp.float32) + 0.5
    ) * step_a
    pos_two = -half_span + (
        (index_b * rows_b + lax.iota(jnp.int32, rows_b)).astype(jnp.float32) + 0.5
    ) * step_b
    heading = (
        -math.pi + (index_c * rows_c + lax.iota(jnp.int32, rows_c)).astype(jnp.float32) * step_c
    ).reshape(rows_c, 1)
    speed_own = 0.5 + ((positions // (N5 * N6)).astype(jnp.float32) + 0.5) * step_four
    speed_other = 0.5 + ((positions // N6 % N5).astype(jnp.float32) + 0.5) * step_five
    drift = jnp.stack(
        [speed_other * jnp.cos(heading) - speed_own, speed_other * jnp.sin(heading)]
    )
    flags = jnp.stack(
        [
            index_a == 0,
            index_a == lax.axis_size("ga") - 1,
            index_b == 0,
            index_b == lax.axis_size("gx") - 1,
        ]
    ).astype(jnp.float32)
    scal = jnp.concatenate([pos_one, pos_two, gust.reshape(-1), flags])

    g4, g5, g6, h_inner, most_inner = call(
        inner_kernel,
        "inner_axes",
        [vmem] * 2,
        [full] * 4 + [pltpu.VMEM((3, 8, LANES), jnp.float32)],
    )(value, jnp.asarray(edge_codes()))
    p1, g1 = call(
        lambda *refs: first_kernel(step_a, *refs),
        "axis_1",
        [smem] + [vmem] * 3,
        [full, full],
    )(scal, value, low_a, high_a)

    slab_b = jax.ShapeDtypeStruct((2, 2, 4, width), jnp.float32)
    send_low_b = call(
        send_kernel,
        "send",
        [vmem] + [hbm] * 3,
        [slab_b, slab_b],
    )(value, low_b, g1, most_inner)
    high_b = [backward(x, "gx") for x in send_low_b]

    m, h_part, g3 = call(
        lambda *refs: third_kernel(step_c, *refs),
        "axis_3",
        [smem] + [vmem] * 6,
        [full] * 3,
    )(scal, value, low_c, high_c, h_inner, p1, drift)

    devices = lax.axis_size(axes)
    inputs = (p1, m, h_part, drift)

    def last(name, lines, upper, ghost, *most):
        part = pltpu.VMEM((len(lines), 2, *value.shape[2:]), jnp.float32)
        final = len(most) > 1
        peaks = (devices, LANES) if final else (3, 4, 256)
        return call(
            lambda *refs: last_kernel(step_b, lines, upper, final, *refs),
            name,
            [smem] + [vmem] * (6 + len(most)),
            [part, part, pltpu.VMEM(peaks, jnp.float32)],
        )(scal, value, ghost, *inputs, *most)

    h0, g20, most = last("rates_0", (0, 1, 2, 3), False, low_b)
    h1, g21, most = last("rates_1", (0, 1), True, high_b[0], most)
    h2, g22, local = last("rates_2", (2, 3), True, high_b[1], most, most_inner)

    spread = lax.all_to_all(local, axes, 0, 0, tiled=True)
    spacings = (step_a, step_b, step_c, step_four, step_five, omega_step)
    value_next, time_step = call(
        lambda *refs: update_kernel(spacings, *refs),
        "update",
        [vmem] * 13,
        [jax.ShapeDtypeStruct(value.shape, jnp.float32), jax.ShapeDtypeStruct((1, 1), jnp.float32)],
    )(value, g1, g3, g4, g5, g6, h0, h1, h2, g20, g21, g22, spread)
    return (value_next, time_step.reshape(1))


def solution(mesh):
    in_specs = (P("ga", "gx", "gy", None), P("ga", "gx"))
    out_specs = (P("ga", "gx", "gy", None), P())
    return jax.shard_map(body, mesh=mesh, in_specs=in_specs, out_specs=out_specs, check_vma=False)
```
